32 devices in a mesh: dp: 4 (over y, x), filter: 8 (over z, core).
Axes of the slice: x: 2, y: 2, z: 4, core: 2. Of those that a mesh axis runs over, the one named last changes fastest.
Arguments:
- fields: bfloat16 [4, 32, 32, 1024], P('dp', None, None, 'filter'), may hold values from -6 to 6
- weight_one: bfloat16 [3, 3, 1024, 1024], P(None, None, 'dp', 'filter'), may hold values from -0.0625 to 0.0625
- weight_two: bfloat16 [3, 3, 1024, 1024], P(None, None, 'dp', 'filter'), may hold values from -0.0625 to 0.0625
- cotangent: bfloat16 [4, 32, 32, 1024], P('dp', None, None, 'filter'), may hold values from -6 to 6
Outputs:
- output: bfloat16 [4, 32, 32, 1024], P('dp', None, None, 'filter')
- grad_one: float32 [3, 3, 1024, 1024], P(None, None, 'dp', 'filter')
- grad_two: float32 [3, 3, 1024, 1024], P(None, None, 'dp', 'filter')
The draws below stay inside these ranges and needn't reach their ends.
All inputs are finite; a program needn't handle non-finite values.
Results may differ from the reference program's by a relative error of at most 0.018.
Values may be sent and summed in bfloat16 or wider, within the bound.
No kernel may reach another device: no remote copies, remote signals or barrier semaphores. Data moves between devices by JAX's collectives and lax.ppermute only.
A program may use at most 128 MiB of HBM per device.

```python
import jax
import jax.numpy as jnp
from jax import lax

C = 1024
CROP = 32
B_DEV = 1
BATCH = 4
N_DP = 4
N_FILTER = 8


def with_spikes(entries, own_key, source, target, parts, factor):
    owner, partner = [(jnp.arange(entries.shape[position]) // (entries.shape[position] // parts)).reshape([-1 if axis == position else 1 for axis in range(entries.ndim)]) for position in (source, target)]
    chosen = jax.random.permutation(own_key, parts)[partner]
    strong = (owner == chosen) | (owner == (partner + parts // 2) % parts)
    return jnp.where(strong, factor * entries, entries)


def block_scale(rng, extent, split, low, largest):
    level, own = 1.0, jax.random.fold_in(rng, 6)
    for dim, blocks in split:
        steps = jnp.exp(jax.random.uniform(jax.random.fold_in(own, dim), (blocks,), jnp.float32, low / len(split), largest / len(split)))
        level = level * jnp.repeat(steps, extent[dim] // blocks).reshape([-1 if axis == dim else 1 for axis in range(len(extent))])
    return level


def bell_draw(own_key, dims, scale, bound, cuts=(), held_as=jnp.bfloat16):
    drawn = jax.random.normal(own_key, dims, jnp.float32) * scale
    if len(cuts) > 0:
        drawn = block_scale(own_key, dims, cuts, -0.22, 0.18) * drawn
    return jnp.clip(drawn, min=-bound, max=bound).astype(held_as)


def gaussian_with(key, dims, spread, bound, cuts, heavy, dtype=jnp.bfloat16):
    values = spread * jax.random.normal(key, dims, jnp.float32)
    if cuts:
        values = values * block_scale(key, dims, cuts, -0.22, 0.18)
    return jnp.clip(with_spikes(values, jax.random.fold_in(key, 3), *heavy), -bound, bound).astype(dtype)


def setup_inputs(seed: int = 0) -> dict:
    streams_of = jax.random.split(jax.random.key(seed), 5)
    fields = gaussian_with(streams_of[0], (BATCH, CROP, CROP, C), 1.0, 6.0, ((0, 4), (3, 8)), (0, 3, 4, 2.0))
    weight_one = bell_draw(streams_of[1], (3, 3, C, C), (9 * C) ** -0.5, 0.0625, ((2, 4), (3, 8)))
    weight_two = bell_draw(streams_of[2], (3, 3, C, C), (9 * C) ** -0.5, 0.0625, ((2, 4), (3, 8)))
    cotangent = bell_draw(streams_of[3], (BATCH, CROP, CROP, C), 1.0, 6.0, ((0, 4), (3, 8)))
    return {"fields": fields, "weight_one": weight_one, "weight_two": weight_two, "cotangent": cotangent}


def conv_taps(inputs, weights):
    size = inputs.shape[1]
    padded = jnp.pad(inputs, ((0, 0), (1, 1), (1, 1), (0, 0)))
    result = jnp.zeros(inputs.shape[:3] + (weights.shape[3],), jnp.float32)
    for row_tap in range(3):
        for col_tap in range(3):
            window = padded[:, row_tap:row_tap + size, col_tap:col_tap + size, :]
            result = result + jnp.einsum("bhwc,cd->bhwd", window, weights[row_tap, col_tap], precision=lax.Precision.HIGHEST)
    return result


def transposed(grads, weights):
    size = grads.shape[1]
    padded = jnp.pad(grads, ((0, 0), (1, 1), (1, 1), (0, 0)))
    result = jnp.zeros(grads.shape[:3] + (weights.shape[2],), jnp.float32)
    for row_tap in range(3):
        for col_tap in range(3):
            window = padded[:, 2 - row_tap:2 - row_tap + size, 2 - col_tap:2 - col_tap + size, :]
            result = result + jnp.einsum("bhwd,cd->bhwc", window, weights[row_tap, col_tap], precision=lax.Precision.HIGHEST)
    return result


def blocked_back(grads, weights, count):
    grad_blocks = jnp.moveaxis(grads.reshape(grads.shape[:3] + (count, grads.shape[3] // count)), 3, 0)
    weight_blocks = jnp.moveaxis(weights.reshape(weights.shape[:3] + (count, weights.shape[3] // count)), 3, 0)

    def add_block(carry, pair):
        part = transposed(pair[0], pair[1]).astype(jnp.bfloat16)
        part = lax.optimization_barrier(part)
        return carry + part.astype(jnp.float32), None

    start = jnp.zeros(grads.shape[:3] + (weights.shape[2],), jnp.float32)
    total, unused = lax.scan(add_block, start, (grad_blocks, weight_blocks))
    return total


def filter_grads(inputs, grads):
    size = inputs.shape[1]
    padded = jnp.pad(inputs, ((0, 0), (1, 1), (1, 1), (0, 0)))
    pieces = []
    for row_tap in range(3):
        for col_tap in range(3):
            window = padded[:, row_tap:row_tap + size, col_tap:col_tap + size, :]
            pieces.append(jnp.einsum("bhwc,bhwd->cd", window, grads, precision=lax.Precision.HIGHEST))
    return jnp.stack(pieces).reshape((3, 3) + pieces[0].shape)


def grouped_grads(inputs, grads):
    shaped_in = inputs.reshape((N_DP, B_DEV) + inputs.shape[1:])
    shaped_gr = grads.reshape((N_DP, B_DEV) + grads.shape[1:])

    def add_group(carry, pair):
        part = filter_grads(pair[0], pair[1]).astype(jnp.bfloat16)
        part = lax.optimization_barrier(part)
        return carry + part.astype(jnp.float32), None

    start = jnp.zeros((3, 3, inputs.shape[3], grads.shape[3]), jnp.float32)
    total, unused = lax.scan(add_group, start, (shaped_in, shaped_gr))
    return total


def reference(fields, weight_one, weight_two, cotangent):
    field_wide = fields.astype(jnp.float32)
    first_w = weight_one.astype(jnp.float32)
    second_w = weight_two.astype(jnp.float32)
    cot_wide = cotangent.astype(jnp.float32)
    pre_one = conv_taps(field_wide, first_w)
    hidden = jax.nn.silu(pre_one).astype(jnp.bfloat16)
    hidden_wide = hidden.astype(jnp.float32)
    output = conv_taps(hidden_wide, second_w).astype(jnp.bfloat16)
    grad_two = grouped_grads(hidden_wide, cot_wide)
    back = blocked_back(cot_wide, second_w, N_FILTER)
    sigma = jax.nn.sigmoid(pre_one)
    back_pre = (back * sigma * (1.0 + pre_one * (1.0 - sigma))).astype(jnp.bfloat16)
    grad_one = grouped_grads(field_wide, back_pre.astype(jnp.float32))
    return output, grad_one, grad_two
```

```python
import jax
import jax.numpy as jnp
from jax import lax
from jax.sharding import PartitionSpec as P


def swap(values, axis, size, flip):
    return lax.ppermute(values, axis, [(i, i ^ flip) for i in range(size)])


def after(values, *earlier):
    return lax.optimization_barrier((values,) + earlier)[0]


def rank_blocks(values, axis, size, flips, dim):
    held = [(0, values)]
    for flip in flips:
        held = held + [(k ^ flip, swap(v, axis, size, flip)) for k, v in held]
    return held


def place(held, axis, dim):
    own = lax.axis_index(axis)
    width = held[0][1].shape[dim]
    shape = list(held[0][1].shape)
    shape[dim] = width * len(held)
    whole = jnp.zeros(shape, held[0][1].dtype)
    for k, piece in held:
        whole = lax.dynamic_update_slice_in_dim(whole, piece, (own ^ k) * width, dim)
    return whole


def bits(size):
    return [1 << n for n in range(size.bit_length() - 1)]


def gather_weights(weights, size):
    if size != 4:
        return place(rank_blocks(weights, "dp", size, bits(size), 2), "dp", 2)
    half = weights.shape[2] // 2
    along_x = swap(weights, "dp", size, 1)
    along_y = swap(weights, "dp", size, 2)
    far_low = swap(along_x[:, :, :half], "dp", size, 2)
    far_high = swap(along_y[:, :, half:], "dp", size, 1)
    far = jnp.concatenate([far_low, far_high], axis=2)
    return place([(0, weights), (1, along_x), (2, along_y), (3, far)], "dp", 2)


def gather_fields(values, size):
    flips = bits(size)
    held = rank_blocks(values, "filter", size, flips[:0:-1], 3)
    stacked = jnp.stack([piece for unused, piece in held])
    other = swap(stacked, "filter", size, 1)
    held = held + [(k ^ 1, other[n]) for n, (k, unused) in enumerate(held)]
    return place(held, "filter", 3)


def fold(pieces, axis, size, flip):
    keep = sorted(k for k in pieces if not k & flip)
    got = swap(jnp.stack([pieces[k | flip] for k in keep]), axis, size, flip)
    return {k: (pieces[k].astype(jnp.float32) + got[n].astype(jnp.float32)).astype(jnp.bfloat16) for n, k in enumerate(keep)}


def scatter_fields(partial, size):
    own = lax.axis_index("filter")
    width = partial.shape[3] // size
    pieces = {k: lax.dynamic_slice_in_dim(partial, (own ^ k) * width, width, 3) for k in range(size)}
    for flip in bits(size):
        pieces = fold(pieces, "filter", size, flip)
    return pieces[0].astype(jnp.float32)


def scatter_weights(partial, size):
    own = lax.axis_index("dp")
    width = partial.shape[2] // size
    pieces = {k: lax.dynamic_slice_in_dim(partial, (own ^ k) * width, width, 2) for k in range(size)}
    if size != 4:
        for flip in bits(size):
            pieces = fold(pieces, "dp", size, flip)
        return pieces[0].astype(jnp.float32)
    half = width // 2
    low = {k: v[:, :, :half] for k, v in pieces.items()}
    high = {k: v[:, :, half:] for k, v in pieces.items()}
    over_x = swap(jnp.stack([low[3], low[1]]), "dp", size, 1)
    over_y = swap(jnp.stack([high[3], high[2]]), "dp", size, 2)
    wide = lambda v: v.astype(jnp.float32)
    low_y = swap((wide(low[2]) + wide(over_x[0])).astype(jnp.bfloat16), "dp", size, 2)
    high_x = swap((wide(high[1]) + wide(over_y[0])).astype(jnp.bfloat16), "dp", size, 1)
    sum_low = wide(low[0]) + wide(over_x[1]) + wide(low_y)
    sum_high = wide(high[0]) + wide(over_y[1]) + wide(high_x)
    return jnp.concatenate([sum_low, sum_high], axis=2)


def shift_cells(values, row_step, col_step):
    size = values.shape[1]
    padded = jnp.pad(values, ((0, 0), (1, 1), (1, 1), (0, 0)))
    return padded[:, 1 + row_step : 1 + row_step + size, 1 + col_step : 1 + col_step + size, :]


def conv_taps(inputs, weights):
    products = jnp.einsum("bhwc,pqcd->bhwpqd", inputs, weights, preferred_element_type=jnp.float32)
    result = jnp.zeros(inputs.shape[:3] + (weights.shape[3],), jnp.float32)
    for row_tap in range(3):
        for col_tap in range(3):
            result = result + shift_cells(
                products[:, :, :, row_tap, col_tap, :], row_tap - 1, col_tap - 1
            )
    return result


def shifted_stack(grads):
    pieces = []
    for row_tap in range(3):
        for col_tap in range(3):
            pieces.append(shift_cells(grads, 1 - row_tap, 1 - col_tap))
    return jnp.stack(pieces, axis=3).reshape(grads.shape[:3] + (3, 3, grads.shape[3]))


def transposed(grads, weights):
    stacked = shifted_stack(grads)
    return jnp.einsum("bhwpqd,pqcd->bhwc", stacked, weights, preferred_element_type=jnp.float32)


def filter_grads(inputs, grads):
    stacked = shifted_stack(grads)
    return jnp.einsum("bhwc,bhwpqd->pqcd", inputs, stacked, preferred_element_type=jnp.float32)


def body(n_dp, n_filter, fields, weight_one, weight_two, cotangent):
    full_one = gather_weights(weight_one, n_dp)
    gathered = gather_fields(fields, n_filter)
    pre_one = conv_taps(gathered, full_one)
    hidden = jax.nn.silu(pre_one).astype(jnp.bfloat16)
    full_two = gather_weights(after(weight_two, full_one), n_dp)
    hidden_all = gather_fields(hidden, n_filter)
    partial_back = transposed(cotangent, full_two)
    output = conv_taps(hidden_all, full_two).astype(jnp.bfloat16)
    grad_two = scatter_weights(filter_grads(hidden_all, cotangent).astype(jnp.bfloat16), n_dp)
    back = scatter_fields(partial_back.astype(jnp.bfloat16), n_filter)
    sigma = jax.nn.sigmoid(pre_one)
    back_pre = (back * sigma * (1.0 + pre_one * (1.0 - sigma))).astype(jnp.bfloat16)
    grad_one = scatter_weights(filter_grads(gathered, back_pre).astype(jnp.bfloat16), n_dp)
    return (output, grad_one, grad_two)


def solution(mesh):
    n_dp, n_filter = mesh.shape["dp"], mesh.shape["filter"]
    placed = (
        P("dp", None, None, "filter"),
        P(None, None, "dp", "filter"),
        P(None, None, "dp", "filter"),
        P("dp", None, None, "filter"),
    )
    return jax.shard_map(
        lambda *arrays: body(n_dp, n_filter, *arrays),
        mesh=mesh,
        in_specs=placed,
        out_specs=(
            P("dp", None, None, "filter"),
            P(None, None, "dp", "filter"),
            P(None, None, "dp", "filter"),
        ),
        check_vma=False,
    )
```

```python
import functools

import jax
import jax.numpy as jnp
from jax import lax
from jax.experimental import pallas as pl
from jax.experimental.pallas import tpu as pltpu
from jax.sharding import PartitionSpec as P

F32, BF16 = jnp.float32, jnp.bfloat16
ANY = pl.BlockSpec(memory_space=pl.ANY)
VMEM = pl.BlockSpec(memory_space=pltpu.VMEM)
SMEM = pl.BlockSpec(memory_space=pltpu.SMEM)


def swap(values, axis, size, flip):
    return lax.ppermute(values, axis, [(i, i ^ flip) for i in range(size)])


def after(values, *earlier):
    return lax.optimization_barrier((values,) + earlier)[0]


def rank_blocks(values, axis, size, flips, dim):
    held = [(0, values)]
    for flip in flips:
        held = held + [(k ^ flip, swap(v, axis, size, flip)) for k, v in held]
    return held


def place(held, axis, dim):
    own = lax.axis_index(axis)
    width = held[0][1].shape[dim]
    shape = list(held[0][1].shape)
    shape[dim] = width * len(held)
    whole = jnp.zeros(shape, held[0][1].dtype)
    for k, piece in held:
        whole = lax.dynamic_update_slice_in_dim(whole, piece, (own ^ k) * width, dim)
    return whole


def bits(size):
    return [1 << n for n in range(size.bit_length() - 1)]


def gather_weights(weights, size):
    if size != 4:
        return place(rank_blocks(weights, "dp", size, bits(size), 2), "dp", 2)
    half = weights.shape[2] // 2
    along_x = swap(weights, "dp", size, 1)
    along_y = swap(weights, "dp", size, 2)
    far_low = swap(along_x[:, :, :half], "dp", size, 2)
    far_high = swap(along_y[:, :, half:], "dp", size, 1)
    far = jnp.concatenate([far_low, far_high], axis=2)
    return place([(0, weights), (1, along_x), (2, along_y), (3, far)], "dp", 2)


def gather_fields(values, size):
    flips = bits(size)
    held = rank_blocks(values, "filter", size, flips[:0:-1], 3)
    stacked = jnp.stack([piece for unused, piece in held])
    other = swap(stacked, "filter", size, 1)
    held = held + [(k ^ 1, other[n]) for n, (k, unused) in enumerate(held)]
    return place(held, "filter", 3)


def fold(pieces, axis, size, flip):
    keep = sorted(k for k in pieces if not k & flip)
    got = swap(jnp.stack([pieces[k | flip] for k in keep]), axis, size, flip)
    return {k: (pieces[k].astype(jnp.float32) + got[n].astype(jnp.float32)).astype(jnp.bfloat16) for n, k in enumerate(keep)}


def scatter_fields(partial, size):
    own = lax.axis_index("filter")
    width = partial.shape[3] // size
    pieces = {k: lax.dynamic_slice_in_dim(partial, (own ^ k) * width, width, 3) for k in range(size)}
    for flip in bits(size):
        pieces = fold(pieces, "filter", size, flip)
    return pieces[0].astype(jnp.float32)


def scatter_weights(partial, size):
    own = lax.axis_index("dp")
    width = partial.shape[2] // size
    pieces = {k: lax.dynamic_slice_in_dim(partial, (own ^ k) * width, width, 2) for k in range(size)}
    if size != 4:
        for flip in bits(size):
            pieces = fold(pieces, "dp", size, flip)
        return pieces[0].astype(jnp.float32)
    half = width // 2
    low = {k: v[:, :, :half] for k, v in pieces.items()}
    high = {k: v[:, :, half:] for k, v in pieces.items()}
    over_x = swap(jnp.stack([low[3], low[1]]), "dp", size, 1)
    over_y = swap(jnp.stack([high[3], high[2]]), "dp", size, 2)
    wide = lambda v: v.astype(jnp.float32)
    low_y = swap((wide(low[2]) + wide(over_x[0])).astype(jnp.bfloat16), "dp", size, 2)
    high_x = swap((wide(high[1]) + wide(over_y[0])).astype(jnp.bfloat16), "dp", size, 1)
    sum_low = wide(low[0]) + wide(over_x[1]) + wide(low_y)
    sum_high = wide(high[0]) + wide(over_y[1]) + wide(high_x)
    return jnp.concatenate([sum_low, sum_high], axis=2)


def shift_cells(values, row_step, col_step):
    size = values.shape[1]
    padded = jnp.pad(values, ((0, 0), (1, 1), (1, 1), (0, 0)))
    return padded[:, 1 + row_step : 1 + row_step + size, 1 + col_step : 1 + col_step + size, :]


def conv_taps(inputs, weights):
    products = jnp.einsum("bhwc,pqcd->bhwpqd", inputs, weights, preferred_element_type=jnp.float32)
    result = jnp.zeros(inputs.shape[:3] + (weights.shape[3],), jnp.float32)
    for row_tap in range(3):
        for col_tap in range(3):
            result = result + shift_cells(
                products[:, :, :, row_tap, col_tap, :], row_tap - 1, col_tap - 1
            )
    return result


def shifted_stack(grads):
    pieces = []
    for row_tap in range(3):
        for col_tap in range(3):
            pieces.append(shift_cells(grads, 1 - row_tap, 1 - col_tap))
    return jnp.stack(pieces, axis=3).reshape(grads.shape[:3] + (3, 3, grads.shape[3]))


def transposed(grads, weights):
    stacked = shifted_stack(grads)
    return jnp.einsum("bhwpqd,pqcd->bhwc", stacked, weights, preferred_element_type=jnp.float32)


def filter_grads(inputs, grads):
    stacked = shifted_stack(grads)
    return jnp.einsum("bhwc,bhwpqd->pqcd", inputs, stacked, preferred_element_type=jnp.float32)


def body(n_dp, n_filter, fields, weight_one, weight_two, cotangent):
    full_one = gather_weights(weight_one, n_dp)
    gathered = gather_fields(fields, n_filter)
    pre_one = conv_taps(gathered, full_one)
    hidden = jax.nn.silu(pre_one).astype(jnp.bfloat16)
    full_two = gather_weights(after(weight_two, full_one), n_dp)
    hidden_all = gather_fields(hidden, n_filter)
    partial_back = transposed(cotangent, full_two)
    output = conv_taps(hidden_all, full_two).astype(jnp.bfloat16)
    grad_two = scatter_weights(filter_grads(hidden_all, cotangent).astype(jnp.bfloat16), n_dp)
    back = scatter_fields(partial_back.astype(jnp.bfloat16), n_filter)
    sigma = jax.nn.sigmoid(pre_one)
    back_pre = (back * sigma * (1.0 + pre_one * (1.0 - sigma))).astype(jnp.bfloat16)
    grad_one = scatter_weights(filter_grads(gathered, back_pre).astype(jnp.bfloat16), n_dp)
    return (output, grad_one, grad_two)


ROWS, COLS, CELLS, WIDE, TALL, TILE = 32, 32, 1024, 128, 256, 256


def kernel_call(kernel, out_shape, in_specs, scratch, flops):
    return pl.pallas_call(
        kernel,
        out_shape=out_shape,
        in_specs=in_specs,
        out_specs=[VMEM] * len(out_shape),
        scratch_shapes=scratch,
        compiler_params=pltpu.CompilerParams(vmem_limit_bytes=56 * 2**20),
        cost_estimate=pl.CostEstimate(flops=flops, bytes_accessed=8 * 2**20, transcendentals=0),
    )


def column(rows):
    return lax.broadcasted_iota(jnp.int32, (rows, WIDE), 0) % COLS


def from_left(values):
    return jnp.where(column(values.shape[0]) == 0, 0.0, pltpu.roll(values, 1, 0))


def from_right(values):
    return jnp.where(column(values.shape[0]) == COLS - 1, 0.0, pltpu.roll(values, values.shape[0] - 1, 0))


def start_all(pairs, sems):
    copies = [pltpu.make_async_copy(src, dst, sems.at[n]) for n, (src, dst) in enumerate(pairs)]
    for copy in copies:
        copy.start()
    return copies


def block(index, size):
    return pl.ds(pl.multiple_of(index * size, size), size)


def weight_pairs(own, refs, whole):
    near, along_x, along_y, low, high = refs
    pairs = [(ref, whole.at[:, :, block(own ^ k, TALL), :]) for k, ref in enumerate((near, along_x, along_y))]
    half = TALL // 2
    far = (own ^ 3) * 2
    return pairs + [(low, whole.at[:, :, block(far, half), :]), (high, whole.at[:, :, block(far + 1, half), :])]


def field_pairs(own, refs, whole):
    pieces = [*refs[:4], *(refs[4].at[n] for n in range(3)), refs[5]]
    flips = (0, 2, 4, 6, 1, 3, 5, 7)
    return [(ref, whole.at[pl.ds(COLS, CELLS), block(own ^ k, WIDE)]) for k, ref in zip(flips, pieces)]


def conv_kernel(first, place, *refs):
    fields, weights = refs[:6], refs[6:11]
    outs, (held, taps, sems) = refs[11:-3], refs[-3:]
    copies = start_all(field_pairs(place[0], fields, held) + weight_pairs(place[1], weights, taps), sems)
    edge = jnp.zeros((COLS, held.shape[1]), BF16)
    held[:COLS, :] = edge
    held[COLS + CELLS :, :] = edge
    for copy in copies:
        copy.wait()
    for start in range(0, CELLS, TILE):
        sums = jnp.zeros((TILE, 3 * WIDE), F32)
        for row_tap in range(3):
            across = jnp.concatenate([taps[row_tap, col_tap] for col_tap in range(3)], axis=1)
            begin = start + row_tap * COLS
            sums = sums + jnp.dot(held[begin : begin + TILE, :], across, preferred_element_type=F32)
        total = sums[:, WIDE : 2 * WIDE] + from_left(sums[:, :WIDE]) + from_right(sums[:, 2 * WIDE :])
        if first:
            outs[0][start : start + TILE, :] = total
            outs[1][start : start + TILE, :] = (total / (1.0 + jnp.exp(-total))).astype(BF16)
        else:
            outs[0][start : start + TILE, :] = total.astype(BF16)


def conv(place, fields, weights, first):
    channels = 8 * WIDE
    out = [jax.ShapeDtypeStruct((CELLS, WIDE), F32)] if first else []
    return kernel_call(
        functools.partial(conv_kernel, first),
        out + [jax.ShapeDtypeStruct((CELLS, WIDE), BF16)],
        [SMEM] + [ANY] * 11,
        [
            pltpu.VMEM((CELLS + 2 * COLS, channels), BF16),
            pltpu.VMEM((3, 3, channels, WIDE), BF16),
            pltpu.SemaphoreType.DMA((13,)),
        ],
        2 * 9 * CELLS * channels * WIDE,
    )(place, *fields, *weights)


def spread(values, shifted):
    edge = jnp.zeros((COLS, 3 * WIDE), BF16)
    shifted[:COLS, :] = edge
    shifted[COLS + CELLS :, :] = edge
    wide = values.astype(F32)
    inside = slice(COLS, COLS + CELLS)
    shifted[inside, :WIDE] = from_right(wide).astype(BF16)
    shifted[inside, WIDE : 2 * WIDE] = values
    shifted[inside, 2 * WIDE :] = from_left(wide).astype(BF16)


def back_kernel(place, grads, *refs):
    weights, (keep, send, shifted, taps, sems) = refs[:5], refs[5:]
    copies = start_all(weight_pairs(place[1], weights, taps), sems)
    spread(grads[...], shifted)
    for copy in copies:
        copy.wait()
    odd = (place[0] & 1) == 1
    for pair in range(4):
        rows = slice(pair * 2 * WIDE, (pair + 1) * 2 * WIDE)
        across = jnp.concatenate([taps[p, q, rows, :] for p in range(3) for q in range(3)], axis=1)
        slot = (place[0] >> 1) ^ pair
        for start in range(0, CELLS, TILE):
            begins = [start + (2 - p) * COLS for p in range(3)]
            stacked = jnp.concatenate([shifted[begin : begin + TILE, :] for begin in begins], axis=1)
            sums = lax.dot_general(stacked, across, (((1,), (1,)), ((), ())), preferred_element_type=F32)
            even_part, odd_part = sums[:, :WIDE], sums[:, WIDE:]
            keep[slot, start : start + TILE, :] = jnp.where(odd, odd_part, even_part).astype(BF16)
            send[slot, start : start + TILE, :] = jnp.where(odd, even_part, odd_part).astype(BF16)


def partial_backs(place, grads, weights):
    return kernel_call(
        back_kernel,
        [jax.ShapeDtypeStruct((4, CELLS, WIDE), BF16)] * 2,
        [SMEM, VMEM] + [ANY] * 5,
        [
            pltpu.VMEM((CELLS + 2 * COLS, 3 * WIDE), BF16),
            pltpu.VMEM((3, 3, 8 * WIDE, WIDE), BF16),
            pltpu.SemaphoreType.DMA((5,)),
        ],
        2 * 9 * CELLS * 8 * WIDE * WIDE,
    )(place, grads, *weights)


def grad_kernel(place, *refs):
    mine, other, grads, (out, held, cots, shifted, sems) = refs[:4], refs[4], refs[5:9], refs[9:]
    mine = [ref if len(ref.shape) == 2 else ref.at[1] for ref in mine]
    grads = [ref if len(ref.shape) == 2 else ref.at[0] for ref in grads]
    core = place[0] & 1
    pairs = []
    for k in range(4):
        pairs.append((mine[k], held.at[k, :, block(core, WIDE)]))
        pairs.append((other.at[k], held.at[k, :, block(1 - core, WIDE)]))
        pairs.append((grads[k], cots.at[k]))
    copies = start_all(pairs, sems)
    for k in range(4):
        for copy in copies[3 * k : 3 * k + 3]:
            copy.wait()
        spread(cots[k], shifted)
        for p in range(3):
            begin = (2 - p) * COLS
            sums = lax.dot_general(
                held[k], shifted[begin : begin + CELLS, :], (((0,), (0,)), ((), ())), preferred_element_type=F32
            )
            for q in range(3):
                part = sums[:, q * WIDE : (q + 1) * WIDE]
                out[p, q] = part if k == 0 else out[p, q] + part


def weight_grads(place, mine, other, grads):
    return kernel_call(
        grad_kernel,
        [jax.ShapeDtypeStruct((3, 3, TALL, WIDE), F32)],
        [SMEM] + [ANY] * 9,
        [
            pltpu.VMEM((4, CELLS, TALL), BF16),
            pltpu.VMEM((4, CELLS, WIDE), BF16),
            pltpu.VMEM((CELLS + 2 * COLS, 3 * WIDE), BF16),
            pltpu.SemaphoreType.DMA((12,)),
        ],
        2 * 9 * CELLS * 8 * WIDE * WIDE,
    )(place, *mine, other, *grads)[0]


def over_dp(values, flip):
    return swap(values, "dp", 4, flip)


def over_filter(values, flip):
    return swap(values, "filter", 8, flip)


def far_weights(along_x, along_y):
    half = TALL // 2
    return over_dp(along_x[:, :, :half], 2), over_dp(along_y[:, :, half:], 1)


def at_owner(stacked, index):
    return lax.dynamic_index_in_dim(stacked, index, 0, keepdims=False)


def together(*values):
    return lax.optimization_barrier(values)


def quick_body(n_dp, n_filter, fields, weight_one, weight_two, cotangent):
    own_filter, own_dp = lax.axis_index("filter"), lax.axis_index("dp")
    place = jnp.stack([own_filter, own_dp]).astype(jnp.int32)
    owner = own_dp ^ (own_filter >> 1)
    fields, cotangent = fields.reshape(CELLS, WIDE), cotangent.reshape(CELLS, WIDE)

    one_x, one_y = over_dp(weight_one, 1), over_dp(weight_one, 2)
    field_far, field_near = over_filter(fields, 4), over_filter(fields, 2)
    one_x, one_y, field_far, field_near = together(one_x, one_y, field_far, field_near)

    one_low, one_high = far_weights(one_x, one_y)
    field_last = over_filter(field_far, 2)
    field_other = over_filter(jnp.stack([fields, field_near, field_far]), 1)
    one_low, one_high, field_last, field_other, weight_two = together(
        one_low, one_high, field_last, field_other, weight_two
    )

    two_x, two_y = over_dp(weight_two, 1), over_dp(weight_two, 2)
    field_rest = over_filter(field_last, 1)
    full_one = (weight_one, one_x, one_y, one_low, one_high)
    pre_one, hidden = conv(place, (fields, field_near, field_far, field_last, field_other, field_rest), full_one, True)
    two_x, two_y, hidden = together(two_x, two_y, hidden)

    hidden_far, hidden_near = over_filter(hidden, 4), over_filter(hidden, 2)
    two_low, two_high = far_weights(two_x, two_y)
    hidden_far, hidden_near, two_low, two_high, cotangent, field_last = together(
        hidden_far, hidden_near, two_low, two_high, cotangent, field_last
    )

    hidden_last = over_filter(hidden_far, 2)
    hidden_other = over_filter(jnp.stack([hidden, hidden_near, hidden_far]), 1)
    field_stack = jnp.stack([fields, field_near, field_far, field_last])
    inputs = [jnp.stack([cotangent, at_owner(field_stack, owner ^ k)]) for k in range(4)]
    inputs = [inputs[0]] + [over_dp(inputs[k], k) for k in (1, 2, 3)]
    full_two = (weight_two, two_x, two_y, two_low, two_high)
    keep, send = partial_backs(place, cotangent, full_two)
    keep, send, hidden_last, hidden_other = together(keep, send, hidden_last, hidden_other)

    got = over_filter(send, 1)
    hidden_rest = over_filter(hidden_last, 1)
    chip = lambda n: keep[n].astype(F32) + got[n].astype(F32)
    chip_three, chip_one = chip(3).astype(BF16), chip(1).astype(BF16)
    chip_three, chip_one, hidden_rest, hidden_last = together(chip_three, chip_one, hidden_rest, hidden_last)
    relayed, nearby = over_filter(chip_three, 2), over_filter(chip_one, 2)
    hidden_stack = jnp.stack([hidden, hidden_near, hidden_far, hidden_last])
    hidden_mine = [at_owner(hidden_stack, owner ^ k) for k in range(4)]
    hidden_mine = [hidden_mine[0]] + [over_dp(hidden_mine[k], k) for k in (1, 2, 3)]
    hidden_parts = (hidden, hidden_near, hidden_far, hidden_last, hidden_other, hidden_rest)
    output = conv(place, hidden_parts, full_two, False)[0]
    relayed, nearby, output, *inputs = together(relayed, nearby, output, *inputs)

    distant = over_filter((chip(2) + relayed.astype(F32)).astype(BF16), 4)
    hidden_swapped = over_filter(jnp.stack(hidden_mine), 1)
    grad_two = weight_grads(place, hidden_mine, hidden_swapped, inputs)
    distant, grad_two = together(distant, grad_two)

    back = chip(0) + nearby.astype(F32) + distant.astype(F32)
    sigma = jax.nn.sigmoid(pre_one)
    back_pre = (back * sigma * (1.0 + pre_one * (1.0 - sigma))).astype(BF16)
    back_all = [back_pre] + [over_dp(back_pre, k) for k in (1, 2, 3)]
    field_swapped = over_filter(jnp.stack([v[1] for v in inputs]), 1)
    grad_one = weight_grads(place, inputs, field_swapped, back_all)
    return (output.reshape(1, ROWS, COLS, WIDE), grad_one, grad_two)


def solution(mesh):
    n_dp, n_filter = mesh.shape["dp"], mesh.shape["filter"]

    def choose(arrays):
        fields, weights = arrays[0].shape, arrays[1].shape
        fits = (n_dp, n_filter) == (4, 8) and fields == (1, 32, 32, 128) and weights == (3, 3, 256, 128)
        return quick_body if fits else body

    placed = (
        P("dp", None, None, "filter"),
        P(None, None, "dp", "filter"),
        P(None, None, "dp", "filter"),
        P("dp", None, None, "filter"),
    )
    return jax.shard_map(
        lambda *arrays: choose(arrays)(n_dp, n_filter, *arrays),
        mesh=mesh,
        in_specs=placed,
        out_specs=(
            P("dp", None, None, "filter"),
            P(None, None, "dp", "filter"),
            P(None, None, "dp", "filter"),
        ),
        check_vma=False,
    )
```

```python
import functools

import jax
import jax.numpy as jnp
from jax import lax
from jax.experimental import pallas as pl
from jax.experimental.pallas import tpu as pltpu
from jax.sharding import PartitionSpec as P

F32, BF16 = jnp.float32, jnp.bfloat16
ANY = pl.BlockSpec(memory_space=pl.ANY)
VMEM = pl.BlockSpec(memory_space=pltpu.VMEM)
SMEM = pl.BlockSpec(memory_space=pltpu.SMEM)


def swap(values, axis, size, flip):
    return lax.ppermute(values, axis, [(i, i ^ flip) for i in range(size)])


def after(values, *earlier):
    return lax.optimization_barrier((values,) + earlier)[0]


def rank_blocks(values, axis, size, flips, dim):
    held = [(0, values)]
    for flip in flips:
        held = held + [(k ^ flip, swap(v, axis, size, flip)) for k, v in held]
    return held


def place(held, axis, dim):
    own = lax.axis_index(axis)
    width = held[0][1].shape[dim]
    shape = list(held[0][1].shape)
    shape[dim] = width * len(held)
    whole = jnp.zeros(shape, held[0][1].dtype)
    for k, piece in held:
        whole = lax.dynamic_update_slice_in_dim(whole, piece, (own ^ k) * width, dim)
    return whole


def bits(size):
    return [1 << n for n in range(size.bit_length() - 1)]


def gather_weights(weights, size):
    if size != 4:
        return place(rank_blocks(weights, "dp", size, bits(size), 2), "dp", 2)
    half = weights.shape[2] // 2
    along_x = swap(weights, "dp", size, 1)
    along_y = swap(weights, "dp", size, 2)
    far_low = swap(along_x[:, :, :half], "dp", size, 2)
    far_high = swap(along_y[:, :, half:], "dp", size, 1)
    far = jnp.concatenate([far_low, far_high], axis=2)
    return place([(0, weights), (1, along_x), (2, along_y), (3, far)], "dp", 2)


def gather_fields(values, size):
    flips = bits(size)
    held = rank_blocks(values, "filter", size, flips[:0:-1], 3)
    stacked = jnp.stack([piece for unused, piece in held])
    other = swap(stacked, "filter", size, 1)
    held = held + [(k ^ 1, other[n]) for n, (k, unused) in enumerate(held)]
    return place(held, "filter", 3)


def fold(pieces, axis, size, flip):
    keep = sorted(k for k in pieces if not k & flip)
    got = swap(jnp.stack([pieces[k | flip] for k in keep]), axis, size, flip)
    return {k: (pieces[k].astype(jnp.float32) + got[n].astype(jnp.float32)).astype(jnp.bfloat16) for n, k in enumerate(keep)}


def scatter_fields(partial, size):
    own = lax.axis_index("filter")
    width = partial.shape[3] // size
    pieces = {k: lax.dynamic_slice_in_dim(partial, (own ^ k) * width, width, 3) for k in range(size)}
    for flip in bits(size):
        pieces = fold(pieces, "filter", size, flip)
    return pieces[0].astype(jnp.float32)


def scatter_weights(partial, size):
    own = lax.axis_index("dp")
    width = partial.shape[2] // size
    pieces = {k: lax.dynamic_slice_in_dim(partial, (own ^ k) * width, width, 2) for k in range(size)}
    if size != 4:
        for flip in bits(size):
            pieces = fold(pieces, "dp", size, flip)
        return pieces[0].astype(jnp.float32)
    half = width // 2
    low = {k: v[:, :, :half] for k, v in pieces.items()}
    high = {k: v[:, :, half:] for k, v in pieces.items()}
    over_x = swap(jnp.stack([low[3], low[1]]), "dp", size, 1)
    over_y = swap(jnp.stack([high[3], high[2]]), "dp", size, 2)
    wide = lambda v: v.astype(jnp.float32)
    low_y = swap((wide(low[2]) + wide(over_x[0])).astype(jnp.bfloat16), "dp", size, 2)
    high_x = swap((wide(high[1]) + wide(over_y[0])).astype(jnp.bfloat16), "dp", size, 1)
    sum_low = wide(low[0]) + wide(over_x[1]) + wide(low_y)
    sum_high = wide(high[0]) + wide(over_y[1]) + wide(high_x)
    return jnp.concatenate([sum_low, sum_high], axis=2)


def shift_cells(values, row_step, col_step):
    size = values.shape[1]
    padded = jnp.pad(values, ((0, 0), (1, 1), (1, 1), (0, 0)))
    return padded[:, 1 + row_step : 1 + row_step + size, 1 + col_step : 1 + col_step + size, :]


def conv_taps(inputs, weights):
    products = jnp.einsum("bhwc,pqcd->bhwpqd", inputs, weights, preferred_element_type=jnp.float32)
    result = jnp.zeros(inputs.shape[:3] + (weights.shape[3],), jnp.float32)
    for row_tap in range(3):
        for col_tap in range(3):
            result = result + shift_cells(
                products[:, :, :, row_tap, col_tap, :], row_tap - 1, col_tap - 1
            )
    return result


def shifted_stack(grads):
    pieces = []
    for row_tap in range(3):
        for col_tap in range(3):
            pieces.append(shift_cells(grads, 1 - row_tap, 1 - col_tap))
    return jnp.stack(pieces, axis=3).reshape(grads.shape[:3] + (3, 3, grads.shape[3]))


def transposed(grads, weights):
    stacked = shifted_stack(grads)
    return jnp.einsum("bhwpqd,pqcd->bhwc", stacked, weights, preferred_element_type=jnp.float32)


def filter_grads(inputs, grads):
    stacked = shifted_stack(grads)
    return jnp.einsum("bhwc,bhwpqd->pqcd", inputs, stacked, preferred_element_type=jnp.float32)


def body(n_dp, n_filter, fields, weight_one, weight_two, cotangent):
    full_one = gather_weights(weight_one, n_dp)
    gathered = gather_fields(fields, n_filter)
    pre_one = conv_taps(gathered, full_one)
    hidden = jax.nn.silu(pre_one).astype(jnp.bfloat16)
    full_two = gather_weights(after(weight_two, full_one), n_dp)
    hidden_all = gather_fields(hidden, n_filter)
    partial_back = transposed(cotangent, full_two)
    output = conv_taps(hidden_all, full_two).astype(jnp.bfloat16)
    grad_two = scatter_weights(filter_grads(hidden_all, cotangent).astype(jnp.bfloat16), n_dp)
    back = scatter_fields(partial_back.astype(jnp.bfloat16), n_filter)
    sigma = jax.nn.sigmoid(pre_one)
    back_pre = (back * sigma * (1.0 + pre_one * (1.0 - sigma))).astype(jnp.bfloat16)
    grad_one = scatter_weights(filter_grads(gathered, back_pre).astype(jnp.bfloat16), n_dp)
    return (output, grad_one, grad_two)


ROWS, COLS, CELLS, WIDE, TALL, TILE = 32, 32, 1024, 128, 256, 256
TAPS = range(3)


def kernel_call(kernel, out_shape, in_specs, scratch, share, out_specs=None, aliases=None):
    return pl.pallas_call(
        kernel,
        out_shape=out_shape,
        in_specs=in_specs,
        out_specs=out_specs or [VMEM] * len(out_shape),
        scratch_shapes=scratch,
        input_output_aliases=aliases or {},
        compiler_params=pltpu.CompilerParams(vmem_limit_bytes=56 * 2**20),
        cost_estimate=pl.CostEstimate(
            flops=int(share * 2 * 9 * CELLS * CELLS * WIDE), bytes_accessed=int(share * 2**23), transcendentals=0
        ),
    )


def bf16(*shape):
    return jax.ShapeDtypeStruct(shape, BF16)


def f32(*shape):
    return jax.ShapeDtypeStruct(shape, F32)


def column(rows):
    return lax.broadcasted_iota(jnp.int32, (rows, WIDE), 0) % COLS


def from_left(values):
    return jnp.where(column(values.shape[0]) == 0, 0.0, pltpu.roll(values, 1, 0))


def from_right(values):
    return jnp.where(column(values.shape[0]) == COLS - 1, 0.0, pltpu.roll(values, values.shape[0] - 1, 0))


def start_all(pairs, sems):
    copies = [pltpu.make_async_copy(src, dst, sems.at[n]) for n, (src, dst) in enumerate(pairs)]
    for copy in copies:
        copy.start()
    return copies


def block(index, size):
    return pl.ds(pl.multiple_of(index * size, size), size)


def weight_pairs(refs, whole, far_only=False):
    half = TALL // 2
    if far_only:
        spans = [(0, half), (half, half)]
    else:
        spans = [(0, TALL), (TALL, TALL), (2 * TALL, TALL), (3 * TALL, half), (3 * TALL + half, half)]
    return [(ref, whole.at[:, :, pl.ds(*span), :]) for ref, span in zip(refs, spans)]


def field_pairs(place, refs, whole):
    pieces = [*refs[:4], *([refs[4].at[n] for n in range(4)] if len(refs) == 5 else refs[4:])]
    pairs = []
    for flip, ref in zip((0, 2, 4, 6, 1, 3, 5, 7), pieces):
        channels = place[0] ^ flip
        spot = (((channels >> 1) ^ place[1]) << 1) + (channels & 1)
        pairs.append((ref, whole.at[pl.ds(COLS, CELLS), block(spot, WIDE)]))
    return pairs


def clear_edges(held):
    edge = jnp.zeros((COLS, held.shape[1]), BF16)
    held[:COLS, :] = edge
    held[COLS + CELLS :, :] = edge


def taps_sum(held, taps, depth, start):
    sums = None
    for p in TAPS:
        across = jnp.concatenate([taps[p, q, :depth] for q in TAPS], axis=1)
        begin = start + p * COLS
        part = jnp.dot(held[begin : begin + TILE, :depth], across, preferred_element_type=F32)
        sums = part if sums is None else sums + part
    return sums[:, WIDE : 2 * WIDE] + from_left(sums[:, :WIDE]) + from_right(sums[:, 2 * WIDE :])


def conv_kernel(layer, count, place, *refs):
    outs = refs[-5:-3] if layer == 0 else refs[-4:-3]
    fields, weights, (held, taps, sems) = refs[:count], refs[count : -3 - len(outs)], refs[-3:]
    copies = start_all(field_pairs(place, fields, held) + weight_pairs(weights, taps), sems)
    clear_edges(held)
    for copy in copies:
        copy.wait()
    for start in range(0, CELLS, TILE):
        rows = slice(start, start + TILE)
        total = taps_sum(held, taps, 4 * TALL, start)
        if layer == 0:
            outs[0][rows, :] = total
            outs[1][rows, :] = (total / (1.0 + jnp.exp(-total))).astype(BF16)
        else:
            outs[0][rows, :] = total.astype(BF16)


def conv(layer, place, fields, weights):
    return kernel_call(
        functools.partial(conv_kernel, layer, len(fields)),
        ([f32(CELLS, WIDE)] if layer == 0 else []) + [bf16(CELLS, WIDE)],
        [SMEM] + [ANY] * (len(fields) + 5),
        [
            pltpu.VMEM((CELLS + 2 * COLS, 4 * TALL), BF16),
            pltpu.VMEM((3, 3, 4 * TALL, WIDE), BF16),
            pltpu.SemaphoreType.DMA((13,)),
        ],
        1,
    )(place, *fields, *weights)


def spread(values, shifted):
    clear_edges(shifted)
    wide = values.astype(F32)
    inside = slice(COLS, COLS + CELLS)
    shifted[inside, :WIDE] = from_right(wide).astype(BF16)
    shifted[inside, WIDE : 2 * WIDE] = values
    shifted[inside, 2 * WIDE :] = from_left(wide).astype(BF16)


def back_tile(shifted, taps, first, start, odd):
    across = jnp.concatenate([taps[p, q, first : first + TALL, :] for p in TAPS for q in TAPS], axis=1)
    begins = [start + (2 - p) * COLS for p in TAPS]
    stacked = jnp.concatenate([shifted[begin : begin + TILE, :] for begin in begins], axis=1)
    sums = lax.dot_general(stacked, across, (((1,), (1,)), ((), ())), preferred_element_type=F32)
    even_part, odd_part = sums[:, :WIDE], sums[:, WIDE:]
    return jnp.where(odd, odd_part, even_part).astype(BF16), jnp.where(odd, even_part, odd_part).astype(BF16)


def back_near_kernel(place, grads, own, along_x, along_y, keep, send, shifted, taps, sems):
    copies = start_all(weight_pairs((own, along_x, along_y), taps), sems)
    spread(grads[...], shifted)
    for copy in copies:
        copy.wait()
    odd = (place[0] & 1) == 1
    for k in range(3):
        slot = (place[0] >> 1) ^ place[1] ^ k
        for start in range(0, CELLS, TILE):
            rows = slice(start, start + TILE)
            keep[slot, rows, :], send[slot, rows, :] = back_tile(shifted, taps, k * TALL, start, odd)


def back_near(place, grads, weights):
    return kernel_call(
        back_near_kernel,
        [bf16(4, CELLS, WIDE)] * 2,
        [SMEM, VMEM] + [ANY] * 3,
        [
            pltpu.VMEM((CELLS + 2 * COLS, 3 * WIDE), BF16),
            pltpu.VMEM((3, 3, 3 * TALL, WIDE), BF16),
            pltpu.SemaphoreType.DMA((3,)),
        ],
        0.75,
    )(place, grads, *weights)


def back_far_kernel(place, grads, low, high, keep_in, send_in, keep, send, parts, shifted, taps, sems):
    copies = start_all(weight_pairs((low, high), taps, True), sems)
    spread(grads[...], shifted)
    for copy in copies:
        copy.wait()
    odd = (place[0] & 1) == 1
    slot = (place[0] >> 1) ^ place[1] ^ 3
    for start in range(0, CELLS, TILE):
        rows = slice(start, start + TILE)
        parts[0, rows, :], parts[1, rows, :] = back_tile(shifted, taps, 0, start, odd)
    outward = [pltpu.make_async_copy(parts.at[n], ref.at[slot], sems.at[2 + n]) for n, ref in enumerate((keep, send))]
    for copy in outward:
        copy.start()
    for copy in outward:
        copy.wait()


def back_far(place, grads, weights, keep, send):
    return kernel_call(
        back_far_kernel,
        [bf16(4, CELLS, WIDE)] * 2,
        [SMEM, VMEM] + [ANY] * 4,
        [
            pltpu.VMEM((2, CELLS, WIDE), BF16),
            pltpu.VMEM((CELLS + 2 * COLS, 3 * WIDE), BF16),
            pltpu.VMEM((3, 3, TALL, WIDE), BF16),
            pltpu.SemaphoreType.DMA((4,)),
        ],
        0.25,
        [ANY, ANY],
        {4: 0, 5: 1},
    )(place, grads, *weights, keep, send)


def grad_kernel(slots, adds, place, *refs):
    count = len(slots)
    mine, other, grads = refs[:count], refs[count], refs[count + 1 : 2 * count + 1]
    before = refs[2 * count + 1] if adds else None
    out, held, cots, shifted, sems = refs[2 * count + 1 + adds :]
    mine = [ref if len(ref.shape) == 2 else ref.at[1] for ref in mine]
    grads = [ref if len(ref.shape) == 2 else ref.at[0] for ref in grads]
    core = place[0] & 1
    pairs = []
    for n, slot in enumerate(slots):
        pairs.append((mine[n], held.at[n, :, block(core, WIDE)]))
        pairs.append((other.at[slot], held.at[n, :, block(1 - core, WIDE)]))
        pairs.append((grads[n], cots.at[n]))
    copies = start_all(pairs, sems)
    for n in range(count):
        for copy in copies[3 * n : 3 * n + 3]:
            copy.wait()
        spread(cots[n], shifted)
        for p in TAPS:
            begin = (2 - p) * COLS
            sums = lax.dot_general(
                held[n], shifted[begin : begin + CELLS, :], (((0,), (0,)), ((), ())), preferred_element_type=F32
            )
            for q in TAPS:
                part = sums[:, q * WIDE : (q + 1) * WIDE]
                earlier = before if n == 0 else out
                out[p, q] = part if earlier is None else earlier[p, q] + part


def weight_grads(place, mine, other, grads, before, slots):
    count = len(slots)
    adds = 0 if before is None else 1
    return kernel_call(
        functools.partial(grad_kernel, slots, adds),
        [f32(3, 3, TALL, WIDE)],
        [SMEM] + [ANY] * (2 * count + 1) + [VMEM] * adds,
        [
            pltpu.VMEM((count, CELLS, TALL), BF16),
            pltpu.VMEM((count, CELLS, WIDE), BF16),
            pltpu.VMEM((CELLS + 2 * COLS, 3 * WIDE), BF16),
            pltpu.SemaphoreType.DMA((3 * count,)),
        ],
        count / 4,
    )(place, *mine, other, *grads, *([] if before is None else [before]))[0]


def over_dp(values, flip, name):
    with jax.named_scope(name):
        return swap(values, "dp", 4, flip)


def over_filter(values, flip, name):
    with jax.named_scope(name):
        return swap(values, "filter", 8, flip)


def together(*values):
    return lax.optimization_barrier(values)


def others(pieces, name):
    return [pieces[0]] + [over_dp(pieces[k], k, name + str(k)) for k in (1, 2, 3)]


def pick(pieces, index):
    chosen = pieces[0]
    for n in (1, 2, 3):
        chosen = jnp.where(index == n, pieces[n], chosen)
    return chosen


def scoped(name, function, *arguments):
    with jax.named_scope(name):
        return function(*arguments)


def quick_body(n_dp, n_filter, fields, weight_one, weight_two, cotangent):
    own_filter, own_dp = lax.axis_index("filter"), lax.axis_index("dp")
    place = jnp.stack([own_filter, own_dp]).astype(jnp.int32)
    owner = own_dp ^ (own_filter >> 1)
    fields, cotangent = fields.reshape(CELLS, WIDE), cotangent.reshape(CELLS, WIDE)

    half = TALL // 2

    def far_weights(along_x, along_y, name):
        return over_dp(along_x[:, :, :half], 2, name + "_low"), over_dp(along_y[:, :, half:], 1, name + "_high")

    one_x, one_y = over_dp(weight_one, 1, "one_x"), over_dp(weight_one, 2, "one_y")
    field_near, field_far = over_filter(fields, 2, "field_near"), over_filter(fields, 4, "field_far")
    field_core0 = over_filter(fields, 1, "field_core0")
    field_near, field_far, one_x, one_y, field_core0, place = together(
        field_near, field_far, one_x, one_y, field_core0, place)
    one_low, one_high = far_weights(one_x, one_y, "one")
    field_last = over_filter(field_far, 2, "field_last")
    field_core1, field_core2 = over_filter(field_near, 1, "field_core1"), over_filter(field_far, 1, "field_core2")
    field_last, field_core1, field_core2, one_low, one_high = together(
        field_last, field_core1, field_core2, one_low, one_high)
    field_core3 = over_filter(field_last, 1, "field_core3")
    field_z = (fields, field_near, field_far, field_last)
    field_core3, weight_gated = together(field_core3, weight_two)
    two_x, two_y = over_dp(weight_gated, 1, "two_x"), over_dp(weight_gated, 2, "two_y")
    pre_one, hidden = scoped(
        "conv_one", conv, 0, place, (*field_z, field_core0, field_core1, field_core2, field_core3),
        (weight_one, one_x, one_y, one_low, one_high)
    )
    hidden_far, hidden_near = over_filter(hidden, 4, "hidden_far"), over_filter(hidden, 2, "hidden_near")
    two_x, two_y, gate, *field_z = together(two_x, two_y, hidden, *field_z)

    two_low, two_high = far_weights(two_x, two_y, "two")
    keep, send = scoped("back_near", back_near, place, cotangent, (weight_two, two_x, two_y))
    inputs = [jnp.stack([cotangent, pick(field_z, owner ^ k)]) for k in range(4)]
    two_low, two_high, keep, send, hidden_far, hidden_near, *inputs = together(
        two_low, two_high, keep, send, hidden_far, hidden_near, *inputs
    )

    inputs = others(inputs, "input")
    hidden_last = over_filter(hidden_far, 2, "hidden_last")
    keep, send = scoped("back_far", back_far, place, cotangent, (two_low, two_high), keep, send)
    got = over_filter(send, 1, "back_core")
    chip = lambda n: keep[n].astype(F32) + got[n].astype(F32)
    chip_one, chip_three = chip(1).astype(BF16), chip(3).astype(BF16)
    relayed = over_filter(chip_three, 2, "relayed")
    hidden_z = (hidden, hidden_near, hidden_far, hidden_last)
    hidden_stack = jnp.stack(hidden_z)
    hidden_picked = [pick(hidden_z, owner ^ k) for k in range(4)]
    chip_two = (chip(2) + relayed.astype(F32)).astype(BF16)
    hidden_core = over_filter(hidden_stack, 1, "hidden_core")
    chip_one, chip_two, *hidden_picked = together(chip_one, chip_two, *hidden_picked)

    distant, nearby = over_filter(chip_two, 4, "distant"), over_filter(chip_one, 2, "nearby")
    full_two = (weight_two, two_x, two_y, two_low, two_high)
    output = scoped("conv_two", conv, 1, place, (*hidden_z, hidden_core), full_two)[0]
    hidden_mine = others(hidden_picked, "hidden_to")
    distant, nearby, output, *rest = together(distant, nearby, output, *hidden_mine, *inputs)
    hidden_mine, inputs = rest[:4], rest[4:]

    field_swapped = over_filter(jnp.stack([v[1] for v in inputs]), 1, "field_swap")
    back = chip(0) + nearby.astype(F32) + distant.astype(F32)
    sigma = jax.nn.sigmoid(pre_one)
    back_pre = (back * sigma * (1.0 + pre_one * (1.0 - sigma))).astype(BF16)
    back_all = others([back_pre] * 4, "pre")
    hidden_swapped = over_filter(jnp.stack(hidden_mine), 1, "hidden_swap")
    grad_two = scoped(
        "grad_two", weight_grads, place, hidden_mine, hidden_swapped, inputs, None, (0, 1, 2, 3)
    )
    grad_one = scoped("grad_one_own", weight_grads, place, inputs[:1], field_swapped, back_all[:1], None, (0,))
    *back_rest, grad_two, grad_one, output = together(*back_all[1:], grad_two, grad_one, output)
    grad_one = scoped(
        "grad_one", weight_grads, place, inputs[1:], field_swapped, back_rest, grad_one, (1, 2, 3)
    )
    return (output.reshape(1, ROWS, COLS, WIDE), grad_one, grad_two)


def solution(mesh):
    n_dp, n_filter = mesh.shape["dp"], mesh.shape["filter"]

    def choose(arrays):
        fields, weights = arrays[0].shape, arrays[1].shape
        fits = (n_dp, n_filter) == (4, 8) and fields == (1, 32, 32, 128) and weights == (3, 3, 256, 128)
        return quick_body if fits else body

    placed = (
        P("dp", None, None, "filter"),
        P(None, None, "dp", "filter"),
        P(None, None, "dp", "filter"),
        P("dp", None, None, "filter"),
    )
    return jax.shard_map(
        lambda *arrays: choose(arrays)(n_dp, n_filter, *arrays),
        mesh=mesh,
        in_specs=placed,
        out_specs=(
            P("dp", None, None, "filter"),
            P(None, None, "dp", "filter"),
            P(None, None, "dp", "filter"),
        ),
        check_vma=False,
    )
```

```python
import functools

import jax
import jax.numpy as jnp
from jax import lax
from jax.experimental import pallas as pl
from jax.experimental.pallas import tpu as pltpu
from jax.sharding import PartitionSpec as P

F32, BF16 = jnp.float32, jnp.bfloat16
ANY = pl.BlockSpec(memory_space=pl.ANY)
VMEM = pl.BlockSpec(memory_space=pltpu.VMEM)
SMEM = pl.BlockSpec(memory_space=pltpu.SMEM)


def swap(values, axis, size, flip):
    return lax.ppermute(values, axis, [(i, i ^ flip) for i in range(size)])


def after(values, *earlier):
    return lax.optimization_barrier((values,) + earlier)[0]


def rank_blocks(values, axis, size, flips, dim):
    held = [(0, values)]
    for flip in flips:
        held = held + [(k ^ flip, swap(v, axis, size, flip)) for k, v in held]
    return held


def place(held, axis, dim):
    own = lax.axis_index(axis)
    width = held[0][1].shape[dim]
    shape = list(held[0][1].shape)
    shape[dim] = width * len(held)
    whole = jnp.zeros(shape, held[0][1].dtype)
    for k, piece in held:
        whole = lax.dynamic_update_slice_in_dim(whole, piece, (own ^ k) * width, dim)
    return whole


def bits(size):
    return [1 << n for n in range(size.bit_length() - 1)]


def gather_weights(weights, size):
    if size != 4:
        return place(rank_blocks(weights, "dp", size, bits(size), 2), "dp", 2)
    half = weights.shape[2] // 2
    along_x = swap(weights, "dp", size, 1)
    along_y = swap(weights, "dp", size, 2)
    far_low = swap(along_x[:, :, :half], "dp", size, 2)
    far_high = swap(along_y[:, :, half:], "dp", size, 1)
    far = jnp.concatenate([far_low, far_high], axis=2)
    return place([(0, weights), (1, along_x), (2, along_y), (3, far)], "dp", 2)


def gather_fields(values, size):
    flips = bits(size)
    held = rank_blocks(values, "filter", size, flips[:0:-1], 3)
    stacked = jnp.stack([piece for unused, piece in held])
    other = swap(stacked, "filter", size, 1)
    held = held + [(k ^ 1, other[n]) for n, (k, unused) in enumerate(held)]
    return place(held, "filter", 3)


def fold(pieces, axis, size, flip):
    keep = sorted(k for k in pieces if not k & flip)
    got = swap(jnp.stack([pieces[k | flip] for k in keep]), axis, size, flip)
    return {k: (pieces[k].astype(jnp.float32) + got[n].astype(jnp.float32)).astype(jnp.bfloat16) for n, k in enumerate(keep)}


def scatter_fields(partial, size):
    own = lax.axis_index("filter")
    width = partial.shape[3] // size
    pieces = {k: lax.dynamic_slice_in_dim(partial, (own ^ k) * width, width, 3) for k in range(size)}
    for flip in bits(size):
        pieces = fold(pieces, "filter", size, flip)
    return pieces[0].astype(jnp.float32)


def scatter_weights(partial, size):
    own = lax.axis_index("dp")
    width = partial.shape[2] // size
    pieces = {k: lax.dynamic_slice_in_dim(partial, (own ^ k) * width, width, 2) for k in range(size)}
    if size != 4:
        for flip in bits(size):
            pieces = fold(pieces, "dp", size, flip)
        return pieces[0].astype(jnp.float32)
    half = width // 2
    low = {k: v[:, :, :half] for k, v in pieces.items()}
    high = {k: v[:, :, half:] for k, v in pieces.items()}
    over_x = swap(jnp.stack([low[3], low[1]]), "dp", size, 1)
    over_y = swap(jnp.stack([high[3], high[2]]), "dp", size, 2)
    wide = lambda v: v.astype(jnp.float32)
    low_y = swap((wide(low[2]) + wide(over_x[0])).astype(jnp.bfloat16), "dp", size, 2)
    high_x = swap((wide(high[1]) + wide(over_y[0])).astype(jnp.bfloat16), "dp", size, 1)
    sum_low = wide(low[0]) + wide(over_x[1]) + wide(low_y)
    sum_high = wide(high[0]) + wide(over_y[1]) + wide(high_x)
    return jnp.concatenate([sum_low, sum_high], axis=2)


def shift_cells(values, row_step, col_step):
    size = values.shape[1]
    padded = jnp.pad(values, ((0, 0), (1, 1), (1, 1), (0, 0)))
    return padded[:, 1 + row_step : 1 + row_step + size, 1 + col_step : 1 + col_step + size, :]


def conv_taps(inputs, weights):
    products = jnp.einsum("bhwc,pqcd->bhwpqd", inputs, weights, preferred_element_type=jnp.float32)
    result = jnp.zeros(inputs.shape[:3] + (weights.shape[3],), jnp.float32)
    for row_tap in range(3):
        for col_tap in range(3):
            result = result + shift_cells(
                products[:, :, :, row_tap, col_tap, :], row_tap - 1, col_tap - 1
            )
    return result


def shifted_stack(grads):
    pieces = []
    for row_tap in range(3):
        for col_tap in range(3):
            pieces.append(shift_cells(grads, 1 - row_tap, 1 - col_tap))
    return jnp.stack(pieces, axis=3).reshape(grads.shape[:3] + (3, 3, grads.shape[3]))


def transposed(grads, weights):
    stacked = shifted_stack(grads)
    return jnp.einsum("bhwpqd,pqcd->bhwc", stacked, weights, preferred_element_type=jnp.float32)


def filter_grads(inputs, grads):
    stacked = shifted_stack(grads)
    return jnp.einsum("bhwc,bhwpqd->pqcd", inputs, stacked, preferred_element_type=jnp.float32)


def body(n_dp, n_filter, fields, weight_one, weight_two, cotangent):
    full_one = gather_weights(weight_one, n_dp)
    gathered = gather_fields(fields, n_filter)
    pre_one = conv_taps(gathered, full_one)
    hidden = jax.nn.silu(pre_one).astype(jnp.bfloat16)
    full_two = gather_weights(after(weight_two, full_one), n_dp)
    hidden_all = gather_fields(hidden, n_filter)
    partial_back = transposed(cotangent, full_two)
    output = conv_taps(hidden_all, full_two).astype(jnp.bfloat16)
    grad_two = scatter_weights(filter_grads(hidden_all, cotangent).astype(jnp.bfloat16), n_dp)
    back = scatter_fields(partial_back.astype(jnp.bfloat16), n_filter)
    sigma = jax.nn.sigmoid(pre_one)
    back_pre = (back * sigma * (1.0 + pre_one * (1.0 - sigma))).astype(jnp.bfloat16)
    grad_one = scatter_weights(filter_grads(gathered, back_pre).astype(jnp.bfloat16), n_dp)
    return (output, grad_one, grad_two)


ROWS, COLS, CELLS, WIDE, TALL, TILE = 32, 32, 1024, 128, 256, 256
TAPS = range(3)


def kernel_call(kernel, out_shape, in_specs, scratch, share, out_specs=None, aliases=None):
    return pl.pallas_call(
        kernel,
        out_shape=out_shape,
        in_specs=in_specs,
        out_specs=out_specs or [VMEM] * len(out_shape),
        scratch_shapes=scratch,
        input_output_aliases=aliases or {},
        compiler_params=pltpu.CompilerParams(vmem_limit_bytes=56 * 2**20),
        cost_estimate=pl.CostEstimate(
            flops=int(share * 2 * 9 * CELLS * CELLS * WIDE), bytes_accessed=int(share * 2**23), transcendentals=0
        ),
    )


def bf16(*shape):
    return jax.ShapeDtypeStruct(shape, BF16)


def f32(*shape):
    return jax.ShapeDtypeStruct(shape, F32)


def column(rows):
    return lax.broadcasted_iota(jnp.int32, (rows, WIDE), 0) % COLS


def from_left(values):
    return jnp.where(column(values.shape[0]) == 0, 0.0, pltpu.roll(values, 1, 0))


def from_right(values):
    return jnp.where(column(values.shape[0]) == COLS - 1, 0.0, pltpu.roll(values, values.shape[0] - 1, 0))


def start_all(pairs, sems):
    copies = [pltpu.make_async_copy(src, dst, sems.at[n]) for n, (src, dst) in enumerate(pairs)]
    for copy in copies:
        copy.start()
    return copies


def block(index, size):
    return pl.ds(pl.multiple_of(index * size, size), size)


def weight_pairs(refs, whole, far_only=False):
    half = TALL // 2
    if far_only:
        spans = [(0, half), (half, half)]
    else:
        spans = [(0, TALL), (TALL, TALL), (2 * TALL, TALL), (3 * TALL, half), (3 * TALL + half, half)]
    return [(ref, whole.at[:, :, pl.ds(*span), :]) for ref, span in zip(refs, spans)]


def field_pairs(place, refs, whole):
    pieces = [*refs[:4], *([refs[4].at[n] for n in range(4)] if len(refs) == 5 else refs[4:])]
    pairs = []
    for flip, ref in zip((0, 2, 4, 6, 1, 3, 5, 7), pieces):
        channels = place[0] ^ flip
        spot = (((channels >> 1) ^ place[1]) << 1) + (channels & 1)
        pairs.append((ref, whole.at[pl.ds(COLS, CELLS), block(spot, WIDE)]))
    return pairs


def clear_edges(held):
    edge = jnp.zeros((COLS, held.shape[1]), BF16)
    held[:COLS, :] = edge
    held[COLS + CELLS :, :] = edge


def taps_sum(held, taps, depth, start):
    sums = None
    for p in TAPS:
        across = jnp.concatenate([taps[p, q, :depth] for q in TAPS], axis=1)
        begin = start + p * COLS
        part = jnp.dot(held[begin : begin + TILE, :depth], across, preferred_element_type=F32)
        sums = part if sums is None else sums + part
    return sums[:, WIDE : 2 * WIDE] + from_left(sums[:, :WIDE]) + from_right(sums[:, 2 * WIDE :])


def conv_kernel(layer, count, place, *refs):
    outs = refs[-5:-3] if layer == 0 else refs[-4:-3]
    fields, weights, (held, taps, sems) = refs[:count], refs[count : -3 - len(outs)], refs[-3:]
    copies = start_all(field_pairs(place, fields, held) + weight_pairs(weights, taps), sems)
    clear_edges(held)
    for copy in copies:
        copy.wait()
    for start in range(0, CELLS, TILE):
        rows = slice(start, start + TILE)
        total = taps_sum(held, taps, 4 * TALL, start)
        if layer == 0:
            outs[0][rows, :] = total
            outs[1][rows, :] = (total / (1.0 + jnp.exp(-total))).astype(BF16)
        else:
            outs[0][rows, :] = total.astype(BF16)


def conv(layer, place, fields, weights):
    return kernel_call(
        functools.partial(conv_kernel, layer, len(fields)),
        ([f32(CELLS, WIDE)] if layer == 0 else []) + [bf16(CELLS, WIDE)],
        [SMEM] + [ANY] * (len(fields) + 5),
        [
            pltpu.VMEM((CELLS + 2 * COLS, 4 * TALL), BF16),
            pltpu.VMEM((3, 3, 4 * TALL, WIDE), BF16),
            pltpu.SemaphoreType.DMA((13,)),
        ],
        1,
    )(place, *fields, *weights)


def spread(values, shifted):
    clear_edges(shifted)
    wide = values.astype(F32)
    inside = slice(COLS, COLS + CELLS)
    shifted[inside, :WIDE] = from_right(wide).astype(BF16)
    shifted[inside, WIDE : 2 * WIDE] = values
    shifted[inside, 2 * WIDE :] = from_left(wide).astype(BF16)


def back_tile(shifted, taps, first, start, odd):
    across = jnp.concatenate([taps[p, q, first : first + TALL, :] for p in TAPS for q in TAPS], axis=1)
    begins = [start + (2 - p) * COLS for p in TAPS]
    stacked = jnp.concatenate([shifted[begin : begin + TILE, :] for begin in begins], axis=1)
    sums = lax.dot_general(stacked, across, (((1,), (1,)), ((), ())), preferred_element_type=F32)
    even_part, odd_part = sums[:, :WIDE], sums[:, WIDE:]
    return jnp.where(odd, odd_part, even_part).astype(BF16), jnp.where(odd, even_part, odd_part).astype(BF16)


def back_near_kernel(place, grads, own, along_x, along_y, keep, send, shifted, taps, sems):
    copies = start_all(weight_pairs((own, along_x, along_y), taps), sems)
    spread(grads[...], shifted)
    for copy in copies:
        copy.wait()
    odd = (place[0] & 1) == 1
    for k in range(3):
        slot = (place[0] >> 1) ^ place[1] ^ k
        for start in range(0, CELLS, TILE):
            rows = slice(start, start + TILE)
            keep[slot, rows, :], send[slot, rows, :] = back_tile(shifted, taps, k * TALL, start, odd)


def back_near(place, grads, weights):
    return kernel_call(
        back_near_kernel,
        [bf16(4, CELLS, WIDE)] * 2,
        [SMEM, VMEM] + [ANY] * 3,
        [
            pltpu.VMEM((CELLS + 2 * COLS, 3 * WIDE), BF16),
            pltpu.VMEM((3, 3, 3 * TALL, WIDE), BF16),
            pltpu.SemaphoreType.DMA((3,)),
        ],
        0.75,
    )(place, grads, *weights)


def back_far_kernel(place, grads, low, high, keep_in, send_in, keep, send, parts, shifted, taps, sems):
    copies = start_all(weight_pairs((low, high), taps, True), sems)
    spread(grads[...], shifted)
    for copy in copies:
        copy.wait()
    odd = (place[0] & 1) == 1
    slot = (place[0] >> 1) ^ place[1] ^ 3
    for start in range(0, CELLS, TILE):
        rows = slice(start, start + TILE)
        parts[0, rows, :], parts[1, rows, :] = back_tile(shifted, taps, 0, start, odd)
    outward = [pltpu.make_async_copy(parts.at[n], ref.at[slot], sems.at[2 + n]) for n, ref in enumerate((keep, send))]
    for copy in outward:
        copy.start()
    for copy in outward:
        copy.wait()


def back_far(place, grads, weights, keep, send):
    return kernel_call(
        back_far_kernel,
        [bf16(4, CELLS, WIDE)] * 2,
        [SMEM, VMEM] + [ANY] * 4,
        [
            pltpu.VMEM((2, CELLS, WIDE), BF16),
            pltpu.VMEM((CELLS + 2 * COLS, 3 * WIDE), BF16),
            pltpu.VMEM((3, 3, TALL, WIDE), BF16),
            pltpu.SemaphoreType.DMA((4,)),
        ],
        0.25,
        [ANY, ANY],
        {4: 0, 5: 1},
    )(place, grads, *weights, keep, send)


def tap_grads(fields, shifted):
    stacked = jnp.concatenate([shifted[(2 - p) * COLS : (2 - p) * COLS + CELLS, :] for p in TAPS], axis=1)
    sums = lax.dot_general(fields, stacked, (((0,), (0,)), ((), ())), preferred_element_type=F32)
    return lambda p, q: sums[:, (3 * p + q) * WIDE : (3 * p + q + 1) * WIDE]


def crop_grad_kernel(count, place, grads, *refs):
    fields, (out_x, out_y, pass_low, pass_high, own, held, shifted, sems) = refs[:count], refs[count:]
    copies = start_all(field_pairs(place, fields, held), sems)
    spread(grads[...], shifted)
    for copy in copies:
        copy.wait()
    half = TALL // 2
    targets = {3: (out_x.at[0], out_y.at[0]), 1: (out_x.at[1], pass_high), 2: (pass_low, out_y.at[1])}
    for k in (3, 1, 2, 0):
        sums = tap_grads(held[COLS : COLS + CELLS, k * TALL : (k + 1) * TALL], shifted)
        for p in TAPS:
            for q in TAPS:
                part = sums(p, q)
                if k == 0:
                    own[p, q] = part
                else:
                    low, high = targets[k]
                    low[p, q] = part[:half].astype(BF16)
                    high[p, q] = part[half:].astype(BF16)


def crop_grads(place, grads, fields):
    half = TALL // 2
    return kernel_call(
        functools.partial(crop_grad_kernel, len(fields)),
        [bf16(2, 3, 3, half, WIDE)] * 2 + [bf16(3, 3, half, WIDE)] * 2 + [f32(3, 3, TALL, WIDE)],
        [SMEM, VMEM] + [ANY] * len(fields),
        [
            pltpu.VMEM((CELLS + 2 * COLS, 4 * TALL), BF16),
            pltpu.VMEM((CELLS + 2 * COLS, 3 * WIDE), BF16),
            pltpu.SemaphoreType.DMA((8,)),
        ],
        1,
    )(place, grads, *fields)


def grad_kernel(slots, adds, place, *refs):
    count = len(slots)
    mine, other, grads = refs[:count], refs[count], refs[count + 1 : 2 * count + 1]
    before = refs[2 * count + 1] if adds else None
    out, held, cots, shifted, sems = refs[2 * count + 1 + adds :]
    core = place[0] & 1
    pairs = []
    for n, slot in enumerate(slots):
        pairs.append((mine[n], held.at[n, :, block(core, WIDE)]))
        pairs.append((other.at[slot], held.at[n, :, block(1 - core, WIDE)]))
        pairs.append((grads[n], cots.at[n]))
    copies = start_all(pairs, sems)
    for n in range(count):
        for copy in copies[3 * n : 3 * n + 3]:
            copy.wait()
        spread(cots[n], shifted)
        sums = tap_grads(held[n], shifted)
        for p in TAPS:
            for q in TAPS:
                earlier = before if n == 0 else out
                out[p, q] = sums(p, q) if earlier is None else earlier[p, q] + sums(p, q)


def weight_grads(place, mine, other, grads, before, slots):
    count = len(slots)
    adds = 0 if before is None else 1
    return kernel_call(
        functools.partial(grad_kernel, slots, adds),
        [f32(3, 3, TALL, WIDE)],
        [SMEM] + [ANY] * (2 * count + 1) + [VMEM] * adds,
        [
            pltpu.VMEM((count, CELLS, TALL), BF16),
            pltpu.VMEM((count, CELLS, WIDE), BF16),
            pltpu.VMEM((CELLS + 2 * COLS, 3 * WIDE), BF16),
            pltpu.SemaphoreType.DMA((3 * count,)),
        ],
        count / 4,
    )(place, *mine, other, *grads, *([] if before is None else [before]))[0]


def over_dp(values, flip, name):
    with jax.named_scope(name):
        return swap(values, "dp", 4, flip)


def over_filter(values, flip, name):
    with jax.named_scope(name):
        return swap(values, "filter", 8, flip)


def together(*values):
    return lax.optimization_barrier(values)


def others(pieces, name):
    return [pieces[0]] + [over_dp(pieces[k], k, name + str(k)) for k in (1, 2, 3)]


def pick(pieces, index):
    chosen = pieces[0]
    for n in (1, 2, 3):
        chosen = jnp.where(index == n, pieces[n], chosen)
    return chosen


def scoped(name, function, *arguments):
    with jax.named_scope(name):
        return function(*arguments)


def quick_body(n_dp, n_filter, fields, weight_one, weight_two, cotangent):
    own_filter, own_dp = lax.axis_index("filter"), lax.axis_index("dp")
    place = jnp.stack([own_filter, own_dp]).astype(jnp.int32)
    owner = own_dp ^ (own_filter >> 1)
    fields, cotangent = fields.reshape(CELLS, WIDE), cotangent.reshape(CELLS, WIDE)

    half = TALL // 2

    def far_weights(along_x, along_y, name):
        return over_dp(along_x[:, :, :half], 2, name + "_low"), over_dp(along_y[:, :, half:], 1, name + "_high")

    one_x, one_y = over_dp(weight_one, 1, "one_x"), over_dp(weight_one, 2, "one_y")
    field_near, field_far = over_filter(fields, 2, "field_near"), over_filter(fields, 4, "field_far")
    field_core0 = over_filter(fields, 1, "field_core0")
    field_near, field_far, one_x, one_y, field_core0, place = together(
        field_near, field_far, one_x, one_y, field_core0, place)
    one_low, one_high = far_weights(one_x, one_y, "one")
    field_last = over_filter(field_far, 2, "field_last")
    field_core1, field_core2 = over_filter(field_near, 1, "field_core1"), over_filter(field_far, 1, "field_core2")
    field_last, field_core1, field_core2, one_low, one_high = together(
        field_last, field_core1, field_core2, one_low, one_high)
    field_core3 = over_filter(field_last, 1, "field_core3")
    field_z = (fields, field_near, field_far, field_last)
    field_core3, weight_gated = together(field_core3, weight_two)
    two_x, two_y = over_dp(weight_gated, 1, "two_x"), over_dp(weight_gated, 2, "two_y")
    pre_one, hidden = scoped(
        "conv_one", conv, 0, place, (*field_z, field_core0, field_core1, field_core2, field_core3),
        (weight_one, one_x, one_y, one_low, one_high)
    )
    hidden_far, hidden_near = over_filter(hidden, 4, "hidden_far"), over_filter(hidden, 2, "hidden_near")
    two_x, two_y, gate, *field_z = together(two_x, two_y, hidden, *field_z)

    two_low, two_high = far_weights(two_x, two_y, "two")
    keep, send = scoped("back_near", back_near, place, cotangent, (weight_two, two_x, two_y))
    inputs = [pick(field_z, owner ^ k) for k in range(4)]
    two_low, two_high, keep, send, hidden_far, hidden_near, *inputs = together(
        two_low, two_high, keep, send, hidden_far, hidden_near, *inputs
    )

    inputs = others(inputs, "input")
    hidden_last = over_filter(hidden_far, 2, "hidden_last")
    keep, send = scoped("back_far", back_far, place, cotangent, (two_low, two_high), keep, send)
    keep, send, hidden_last = together(keep, send, hidden_last)
    got = over_filter(send, 1, "back_core")
    chip = lambda n: keep[n].astype(F32) + got[n].astype(F32)
    chip_one, chip_three = chip(1).astype(BF16), chip(3).astype(BF16)
    relayed = over_filter(chip_three, 2, "relayed")
    hidden_z = (hidden, hidden_near, hidden_far, hidden_last)
    hidden_core = over_filter(jnp.stack(hidden_z), 1, "hidden_core")
    out_x, out_y, pass_low, pass_high, own = scoped(
        "crop_grads", crop_grads, place, cotangent, (*hidden_z, hidden_core)
    )
    chip_two = (chip(2) + relayed.astype(F32)).astype(BF16)
    chip_one, chip_two, out_x, out_y, *inputs = together(chip_one, chip_two, out_x, out_y, *inputs)

    distant, nearby = over_filter(chip_two, 4, "distant"), over_filter(chip_one, 2, "nearby")
    got_x, got_y = over_dp(out_x, 1, "grad_x"), over_dp(out_y, 2, "grad_y")
    full_two = (weight_two, two_x, two_y, two_low, two_high)
    output = scoped("conv_two", conv, 1, place, (*hidden_z, hidden_core), full_two)[0]
    distant, nearby, output = together(distant, nearby, output)

    field_swapped = over_filter(jnp.stack(inputs), 1, "field_swap")
    back = chip(0) + nearby.astype(F32) + distant.astype(F32)
    sigma = jax.nn.sigmoid(pre_one)
    back_pre = (back * sigma * (1.0 + pre_one * (1.0 - sigma))).astype(BF16)
    back_all = others([back_pre] * 4, "pre")
    grad_one = scoped("grad_one_own", weight_grads, place, inputs[:1], field_swapped, back_all[:1], None, (0,))
    wide = lambda value: value.astype(F32)
    to_y = (wide(pass_low) + wide(got_x[0])).astype(BF16)
    to_x = (wide(pass_high) + wide(got_y[0])).astype(BF16)
    last_low, last_high = over_dp(to_y, 2, "grad_low"), over_dp(to_x, 1, "grad_high")
    grad_one, *back_rest = together(grad_one, *back_all[1:])
    grad_one = scoped(
        "grad_one", weight_grads, place, inputs[1:], field_swapped, back_rest, grad_one, (1, 2, 3)
    )
    half = TALL // 2
    grad_two = own + jnp.concatenate(
        [wide(got_x[1]) + wide(last_low), wide(got_y[1]) + wide(last_high)], axis=2
    )
    return (output.reshape(1, ROWS, COLS, WIDE), grad_one, grad_two)


def solution(mesh):
    n_dp, n_filter = mesh.shape["dp"], mesh.shape["filter"]

    def choose(arrays):
        fields, weights = arrays[0].shape, arrays[1].shape
        fits = (n_dp, n_filter) == (4, 8) and fields == (1, 32, 32, 128) and weights == (3, 3, 256, 128)
        return quick_body if fits else body

    placed = (
        P("dp", None, None, "filter"),
        P(None, None, "dp", "filter"),
        P(None, None, "dp", "filter"),
        P("dp", None, None, "filter"),
    )
    return jax.shard_map(
        lambda *arrays: choose(arrays)(n_dp, n_filter, *arrays),
        mesh=mesh,
        in_specs=placed,
        out_specs=(
            P("dp", None, None, "filter"),
            P(None, None, "dp", "filter"),
            P(None, None, "dp", "filter"),
        ),
        check_vma=False,
    )
```

```python
import functools

import jax
import jax.numpy as jnp
from jax import lax
from jax.experimental import pallas as pl
from jax.experimental.pallas import tpu as pltpu
from jax.sharding import PartitionSpec as P

F32, BF16 = jnp.float32, jnp.bfloat16
ANY = pl.BlockSpec(memory_space=pl.ANY)
VMEM = pl.BlockSpec(memory_space=pltpu.VMEM)
SMEM = pl.BlockSpec(memory_space=pltpu.SMEM)


def swap(values, axis, size, flip):
    return lax.ppermute(values, axis, [(i, i ^ flip) for i in range(size)])


def after(values, *earlier):
    return lax.optimization_barrier((values,) + earlier)[0]


def rank_blocks(values, axis, size, flips, dim):
    held = [(0, values)]
    for flip in flips:
        held = held + [(k ^ flip, swap(v, axis, size, flip)) for k, v in held]
    return held


def place(held, axis, dim):
    own = lax.axis_index(axis)
    width = held[0][1].shape[dim]
    shape = list(held[0][1].shape)
    shape[dim] = width * len(held)
    whole = jnp.zeros(shape, held[0][1].dtype)
    for k, piece in held:
        whole = lax.dynamic_update_slice_in_dim(whole, piece, (own ^ k) * width, dim)
    return whole


def bits(size):
    return [1 << n for n in range(size.bit_length() - 1)]


def gather_weights(weights, size):
    if size != 4:
        return place(rank_blocks(weights, "dp", size, bits(size), 2), "dp", 2)
    half = weights.shape[2] // 2
    along_x = swap(weights, "dp", size, 1)
    along_y = swap(weights, "dp", size, 2)
    far_low = swap(along_x[:, :, :half], "dp", size, 2)
    far_high = swap(along_y[:, :, half:], "dp", size, 1)
    far = jnp.concatenate([far_low, far_high], axis=2)
    return place([(0, weights), (1, along_x), (2, along_y), (3, far)], "dp", 2)


def gather_fields(values, size):
    flips = bits(size)
    held = rank_blocks(values, "filter", size, flips[:0:-1], 3)
    stacked = jnp.stack([piece for unused, piece in held])
    other = swap(stacked, "filter", size, 1)
    held = held + [(k ^ 1, other[n]) for n, (k, unused) in enumerate(held)]
    return place(held, "filter", 3)


def fold(pieces, axis, size, flip):
    keep = sorted(k for k in pieces if not k & flip)
    got = swap(jnp.stack([pieces[k | flip] for k in keep]), axis, size, flip)
    return {k: (pieces[k].astype(jnp.float32) + got[n].astype(jnp.float32)).astype(jnp.bfloat16) for n, k in enumerate(keep)}


def scatter_fields(partial, size):
    own = lax.axis_index("filter")
    width = partial.shape[3] // size
    pieces = {k: lax.dynamic_slice_in_dim(partial, (own ^ k) * width, width, 3) for k in range(size)}
    for flip in bits(size):
        pieces = fold(pieces, "filter", size, flip)
    return pieces[0].astype(jnp.float32)


def scatter_weights(partial, size):
    own = lax.axis_index("dp")
    width = partial.shape[2] // size
    pieces = {k: lax.dynamic_slice_in_dim(partial, (own ^ k) * width, width, 2) for k in range(size)}
    if size != 4:
        for flip in bits(size):
            pieces = fold(pieces, "dp", size, flip)
        return pieces[0].astype(jnp.float32)
    half = width // 2
    low = {k: v[:, :, :half] for k, v in pieces.items()}
    high = {k: v[:, :, half:] for k, v in pieces.items()}
    over_x = swap(jnp.stack([low[3], low[1]]), "dp", size, 1)
    over_y = swap(jnp.stack([high[3], high[2]]), "dp", size, 2)
    wide = lambda v: v.astype(jnp.float32)
    low_y = swap((wide(low[2]) + wide(over_x[0])).astype(jnp.bfloat16), "dp", size, 2)
    high_x = swap((wide(high[1]) + wide(over_y[0])).astype(jnp.bfloat16), "dp", size, 1)
    sum_low = wide(low[0]) + wide(over_x[1]) + wide(low_y)
    sum_high = wide(high[0]) + wide(over_y[1]) + wide(high_x)
    return jnp.concatenate([sum_low, sum_high], axis=2)


def shift_cells(values, row_step, col_step):
    size = values.shape[1]
    padded = jnp.pad(values, ((0, 0), (1, 1), (1, 1), (0, 0)))
    return padded[:, 1 + row_step : 1 + row_step + size, 1 + col_step : 1 + col_step + size, :]


def conv_taps(inputs, weights):
    products = jnp.einsum("bhwc,pqcd->bhwpqd", inputs, weights, preferred_element_type=jnp.float32)
    result = jnp.zeros(inputs.shape[:3] + (weights.shape[3],), jnp.float32)
    for row_tap in range(3):
        for col_tap in range(3):
            result = result + shift_cells(
                products[:, :, :, row_tap, col_tap, :], row_tap - 1, col_tap - 1
            )
    return result


def shifted_stack(grads):
    pieces = []
    for row_tap in range(3):
        for col_tap in range(3):
            pieces.append(shift_cells(grads, 1 - row_tap, 1 - col_tap))
    return jnp.stack(pieces, axis=3).reshape(grads.shape[:3] + (3, 3, grads.shape[3]))


def transposed(grads, weights):
    stacked = shifted_stack(grads)
    return jnp.einsum("bhwpqd,pqcd->bhwc", stacked, weights, preferred_element_type=jnp.float32)


def filter_grads(inputs, grads):
    stacked = shifted_stack(grads)
    return jnp.einsum("bhwc,bhwpqd->pqcd", inputs, stacked, preferred_element_type=jnp.float32)


def body(n_dp, n_filter, fields, weight_one, weight_two, cotangent):
    full_one = gather_weights(weight_one, n_dp)
    gathered = gather_fields(fields, n_filter)
    pre_one = conv_taps(gathered, full_one)
    hidden = jax.nn.silu(pre_one).astype(jnp.bfloat16)
    full_two = gather_weights(after(weight_two, full_one), n_dp)
    hidden_all = gather_fields(hidden, n_filter)
    partial_back = transposed(cotangent, full_two)
    output = conv_taps(hidden_all, full_two).astype(jnp.bfloat16)
    grad_two = scatter_weights(filter_grads(hidden_all, cotangent).astype(jnp.bfloat16), n_dp)
    back = scatter_fields(partial_back.astype(jnp.bfloat16), n_filter)
    sigma = jax.nn.sigmoid(pre_one)
    back_pre = (back * sigma * (1.0 + pre_one * (1.0 - sigma))).astype(jnp.bfloat16)
    grad_one = scatter_weights(filter_grads(gathered, back_pre).astype(jnp.bfloat16), n_dp)
    return (output, grad_one, grad_two)


ROWS, COLS, CELLS, WIDE, TALL, TILE = 32, 32, 1024, 128, 256, 256
TAPS = range(3)


def kernel_call(kernel, out_shape, in_specs, scratch, share, out_specs=None, aliases=None):
    return pl.pallas_call(
        kernel,
        out_shape=out_shape,
        in_specs=in_specs,
        out_specs=out_specs or [VMEM] * len(out_shape),
        scratch_shapes=scratch,
        input_output_aliases=aliases or {},
        compiler_params=pltpu.CompilerParams(vmem_limit_bytes=56 * 2**20),
        cost_estimate=pl.CostEstimate(
            flops=int(share * 2 * 9 * CELLS * CELLS * WIDE), bytes_accessed=int(share * 2**23), transcendentals=0
        ),
    )


def bf16(*shape):
    return jax.ShapeDtypeStruct(shape, BF16)


def f32(*shape):
    return jax.ShapeDtypeStruct(shape, F32)


def column(rows):
    return lax.broadcasted_iota(jnp.int32, (rows, WIDE), 0) % COLS


def from_left(values):
    return jnp.where(column(values.shape[0]) == 0, 0.0, pltpu.roll(values, 1, 0))


def from_right(values):
    return jnp.where(column(values.shape[0]) == COLS - 1, 0.0, pltpu.roll(values, values.shape[0] - 1, 0))


def start_all(pairs, sems):
    copies = [pltpu.make_async_copy(src, dst, sems.at[n]) for n, (src, dst) in enumerate(pairs)]
    for copy in copies:
        copy.start()
    return copies


def block(index, size):
    return pl.ds(pl.multiple_of(index * size, size), size)


def weight_pairs(refs, whole, far_only=False):
    half = TALL // 2
    if far_only:
        spans = [(0, half), (half, half)]
    else:
        spans = [(0, TALL), (TALL, TALL), (2 * TALL, TALL), (3 * TALL, half), (3 * TALL + half, half)]
    return [(ref, whole.at[:, :, pl.ds(*span), :]) for ref, span in zip(refs, spans)]


def field_pairs(place, refs, whole):
    pieces = [*refs[:4], *([refs[4].at[n] for n in range(4)] if len(refs) == 5 else refs[4:])]
    pairs = []
    for flip, ref in zip((0, 2, 4, 6, 1, 3, 5, 7), pieces):
        channels = place[0] ^ flip
        spot = (((channels >> 1) ^ place[1]) << 1) + (channels & 1)
        pairs.append((ref, whole.at[pl.ds(COLS, CELLS), block(spot, WIDE)]))
    return pairs


def clear_edges(held):
    edge = jnp.zeros((COLS, held.shape[1]), BF16)
    held[:COLS, :] = edge
    held[COLS + CELLS :, :] = edge


def taps_sum(held, taps, depth, start):
    sums = None
    for p in TAPS:
        across = jnp.concatenate([taps[p, q, :depth] for q in TAPS], axis=1)
        begin = start + p * COLS
        part = jnp.dot(held[begin : begin + TILE, :depth], across, preferred_element_type=F32)
        sums = part if sums is None else sums + part
    return sums[:, WIDE : 2 * WIDE] + from_left(sums[:, :WIDE]) + from_right(sums[:, 2 * WIDE :])


def conv_kernel(layer, count, place, *refs):
    outs = refs[-5:-3] if layer == 0 else refs[-4:-3]
    fields, weights, (held, taps, sems) = refs[:count], refs[count : -3 - len(outs)], refs[-3:]
    copies = start_all(field_pairs(place, fields, held) + weight_pairs(weights, taps), sems)
    clear_edges(held)
    for copy in copies:
        copy.wait()
    for start in range(0, CELLS, TILE):
        rows = slice(start, start + TILE)
        total = taps_sum(held, taps, 4 * TALL, start)
        if layer == 0:
            outs[0][rows, :] = total
            outs[1][rows, :] = (total / (1.0 + jnp.exp(-total))).astype(BF16)
        else:
            outs[0][rows, :] = total.astype(BF16)


def conv(layer, place, fields, weights):
    return kernel_call(
        functools.partial(conv_kernel, layer, len(fields)),
        ([f32(CELLS, WIDE)] if layer == 0 else []) + [bf16(CELLS, WIDE)],
        [SMEM] + [ANY] * (len(fields) + 5),
        [
            pltpu.VMEM((CELLS + 2 * COLS, 4 * TALL), BF16),
            pltpu.VMEM((3, 3, 4 * TALL, WIDE), BF16),
            pltpu.SemaphoreType.DMA((13,)),
        ],
        1,
    )(place, *fields, *weights)


def spread(values, shifted):
    clear_edges(shifted)
    wide = values.astype(F32)
    inside = slice(COLS, COLS + CELLS)
    shifted[inside, :WIDE] = from_right(wide).astype(BF16)
    shifted[inside, WIDE : 2 * WIDE] = values
    shifted[inside, 2 * WIDE :] = from_left(wide).astype(BF16)


def back_tile(shifted, taps, first, start, odd):
    across = jnp.concatenate([taps[p, q, first : first + TALL, :] for p in TAPS for q in TAPS], axis=1)
    begins = [start + (2 - p) * COLS for p in TAPS]
    stacked = jnp.concatenate([shifted[begin : begin + TILE, :] for begin in begins], axis=1)
    sums = lax.dot_general(stacked, across, (((1,), (1,)), ((), ())), preferred_element_type=F32)
    even_part, odd_part = sums[:, :WIDE], sums[:, WIDE:]
    return jnp.where(odd, odd_part, even_part).astype(BF16), jnp.where(odd, even_part, odd_part).astype(BF16)


def back_near_kernel(place, grads, own, along_x, along_y, keep, send, shifted, taps, sems):
    copies = start_all(weight_pairs((own, along_x, along_y), taps), sems)
    spread(grads[...], shifted)
    for copy in copies:
        copy.wait()
    odd = (place[0] & 1) == 1
    for k in range(3):
        slot = (place[0] >> 1) ^ place[1] ^ k
        for start in range(0, CELLS, TILE):
            rows = slice(start, start + TILE)
            keep[slot, rows, :], send[slot, rows, :] = back_tile(shifted, taps, k * TALL, start, odd)


def back_near(place, grads, weights):
    return kernel_call(
        back_near_kernel,
        [bf16(4, CELLS, WIDE)] * 2,
        [SMEM, VMEM] + [ANY] * 3,
        [
            pltpu.VMEM((CELLS + 2 * COLS, 3 * WIDE), BF16),
            pltpu.VMEM((3, 3, 3 * TALL, WIDE), BF16),
            pltpu.SemaphoreType.DMA((3,)),
        ],
        0.75,
    )(place, grads, *weights)


def back_far_kernel(place, grads, low, high, keep_in, send_in, keep, send, parts, shifted, taps, sems):
    copies = start_all(weight_pairs((low, high), taps, True), sems)
    spread(grads[...], shifted)
    for copy in copies:
        copy.wait()
    odd = (place[0] & 1) == 1
    slot = (place[0] >> 1) ^ place[1] ^ 3
    for start in range(0, CELLS, TILE):
        rows = slice(start, start + TILE)
        parts[0, rows, :], parts[1, rows, :] = back_tile(shifted, taps, 0, start, odd)
    outward = [pltpu.make_async_copy(parts.at[n], ref.at[slot], sems.at[2 + n]) for n, ref in enumerate((keep, send))]
    for copy in outward:
        copy.start()
    for copy in outward:
        copy.wait()


def back_far(place, grads, weights, keep, send):
    return kernel_call(
        back_far_kernel,
        [bf16(4, CELLS, WIDE)] * 2,
        [SMEM, VMEM] + [ANY] * 4,
        [
            pltpu.VMEM((2, CELLS, WIDE), BF16),
            pltpu.VMEM((CELLS + 2 * COLS, 3 * WIDE), BF16),
            pltpu.VMEM((3, 3, TALL, WIDE), BF16),
            pltpu.SemaphoreType.DMA((4,)),
        ],
        0.25,
        [ANY, ANY],
        {4: 0, 5: 1},
    )(place, grads, *weights, keep, send)


def tap_grads(fields, shifted):
    stacked = jnp.concatenate([shifted[(2 - p) * COLS : (2 - p) * COLS + CELLS, :] for p in TAPS], axis=1)
    sums = lax.dot_general(fields, stacked, (((0,), (0,)), ((), ())), preferred_element_type=F32)
    return lambda p, q: sums[:, (3 * p + q) * WIDE : (3 * p + q + 1) * WIDE]


def crop_grad_kernel(count, place, grads, *refs):
    fields, (out_x, out_y, pass_low, pass_high, own, held, shifted, sems) = refs[:count], refs[count:]
    copies = start_all(field_pairs(place, fields, held), sems)
    spread(grads[...], shifted)
    for copy in copies:
        copy.wait()
    half = TALL // 2
    targets = {3: (out_x.at[0], out_y.at[0]), 1: (out_x.at[1], pass_high), 2: (pass_low, out_y.at[1])}
    for k in (3, 1, 2, 0):
        sums = tap_grads(held[COLS : COLS + CELLS, k * TALL : (k + 1) * TALL], shifted)
        for p in TAPS:
            for q in TAPS:
                part = sums(p, q)
                if k == 0:
                    own[p, q] = part
                else:
                    low, high = targets[k]
                    low[p, q] = part[:half].astype(BF16)
                    high[p, q] = part[half:].astype(BF16)


def crop_grads(place, grads, fields):
    half = TALL // 2
    return kernel_call(
        functools.partial(crop_grad_kernel, len(fields)),
        [bf16(2, 3, 3, half, WIDE)] * 2 + [bf16(3, 3, half, WIDE)] * 2 + [f32(3, 3, TALL, WIDE)],
        [SMEM, VMEM] + [ANY] * len(fields),
        [
            pltpu.VMEM((CELLS + 2 * COLS, 4 * TALL), BF16),
            pltpu.VMEM((CELLS + 2 * COLS, 3 * WIDE), BF16),
            pltpu.SemaphoreType.DMA((8,)),
        ],
        1,
    )(place, grads, *fields)


def grad_kernel(slots, adds, place, *refs):
    count = len(slots)
    mine, other, grads = refs[:count], refs[count], refs[count + 1 : 2 * count + 1]
    before = refs[2 * count + 1] if adds else None
    out, held, cots, shifted, sems = refs[2 * count + 1 + adds :]
    core = place[0] & 1
    pairs = []
    for n, slot in enumerate(slots):
        pairs.append((mine[n], held.at[n, :, block(core, WIDE)]))
        pairs.append((other.at[slot], held.at[n, :, block(1 - core, WIDE)]))
        pairs.append((grads[n], cots.at[n]))
    copies = start_all(pairs, sems)
    for n in range(count):
        for copy in copies[3 * n : 3 * n + 3]:
            copy.wait()
        spread(cots[n], shifted)
        sums = tap_grads(held[n], shifted)
        for p in TAPS:
            for q in TAPS:
                earlier = before if n == 0 else out
                out[p, q] = sums(p, q) if earlier is None else earlier[p, q] + sums(p, q)


def weight_grads(place, mine, other, grads, before, slots):
    count = len(slots)
    adds = 0 if before is None else 1
    return kernel_call(
        functools.partial(grad_kernel, slots, adds),
        [f32(3, 3, TALL, WIDE)],
        [SMEM] + [ANY] * (2 * count + 1) + [VMEM] * adds,
        [
            pltpu.VMEM((count, CELLS, TALL), BF16),
            pltpu.VMEM((count, CELLS, WIDE), BF16),
            pltpu.VMEM((CELLS + 2 * COLS, 3 * WIDE), BF16),
            pltpu.SemaphoreType.DMA((3 * count,)),
        ],
        count / 4,
    )(place, *mine, other, *grads, *([] if before is None else [before]))[0]


def over_dp(values, flip, name):
    with jax.named_scope(name):
        return swap(values, "dp", 4, flip)


def over_filter(values, flip, name):
    with jax.named_scope(name):
        return swap(values, "filter", 8, flip)


def together(*values):
    return lax.optimization_barrier(values)


def others(pieces, name):
    return [pieces[0]] + [over_dp(pieces[k], k, name + str(k)) for k in (1, 2, 3)]


def pick(pieces, index):
    chosen = pieces[0]
    for n in (1, 2, 3):
        chosen = jnp.where(index == n, pieces[n], chosen)
    return chosen


def scoped(name, function, *arguments):
    with jax.named_scope(name):
        return function(*arguments)


def quick_body(n_dp, n_filter, fields, weight_one, weight_two, cotangent):
    own_filter, own_dp = lax.axis_index("filter"), lax.axis_index("dp")
    place = jnp.stack([own_filter, own_dp]).astype(jnp.int32)
    owner = own_dp ^ (own_filter >> 1)
    fields, cotangent = fields.reshape(CELLS, WIDE), cotangent.reshape(CELLS, WIDE)

    half = TALL // 2

    def far_weights(along_x, along_y, name):
        return over_dp(along_x[:, :, :half], 2, name + "_low"), over_dp(along_y[:, :, half:], 1, name + "_high")

    one_x, one_y = over_dp(weight_one, 1, "one_x"), over_dp(weight_one, 2, "one_y")
    field_near, field_far = over_filter(fields, 2, "field_near"), over_filter(fields, 4, "field_far")
    field_core0 = over_filter(fields, 1, "field_core0")
    field_near, field_far, one_x, one_y, field_core0, place = together(
        field_near, field_far, one_x, one_y, field_core0, place)
    one_low, one_high = far_weights(one_x, one_y, "one")
    field_last = over_filter(field_far, 2, "field_last")
    field_core1, field_core2 = over_filter(field_near, 1, "field_core1"), over_filter(field_far, 1, "field_core2")
    field_last, field_core1, field_core2, one_low, one_high, weight_gated = together(
        field_last, field_core1, field_core2, one_low, one_high, weight_two)
    field_core3 = over_filter(field_last, 1, "field_core3")
    field_z = (fields, field_near, field_far, field_last)
    two_x, two_y = over_dp(weight_gated, 1, "two_x"), over_dp(weight_gated, 2, "two_y")
    pre_one, hidden = scoped(
        "conv_one", conv, 0, place, (*field_z, field_core0, field_core1, field_core2, field_core3),
        (weight_one, one_x, one_y, one_low, one_high)
    )
    hidden_far, hidden_near = over_filter(hidden, 4, "hidden_far"), over_filter(hidden, 2, "hidden_near")
    two_x, two_y, gate, *field_z = together(two_x, two_y, hidden, *field_z)

    two_low, two_high = far_weights(two_x, two_y, "two")
    keep, send = scoped("back_near", back_near, place, cotangent, (weight_two, two_x, two_y))
    inputs = [pick(field_z, owner ^ k) for k in range(4)]
    two_low, two_high, keep, send, hidden_far, hidden_near, *inputs = together(
        two_low, two_high, keep, send, hidden_far, hidden_near, *inputs
    )

    inputs = others(inputs, "input")
    hidden_last = over_filter(hidden_far, 2, "hidden_last")
    keep, send = scoped("back_far", back_far, place, cotangent, (two_low, two_high), keep, send)
    keep, send, hidden_last = together(keep, send, hidden_last)
    got = over_filter(send, 1, "back_core")
    chip = lambda n: keep[n].astype(F32) + got[n].astype(F32)
    chip_one, chip_three = chip(1).astype(BF16), chip(3).astype(BF16)
    relayed = over_filter(chip_three, 2, "relayed")
    hidden_z = (hidden, hidden_near, hidden_far, hidden_last)
    hidden_core = over_filter(jnp.stack(hidden_z), 1, "hidden_core")
    out_x, out_y, pass_low, pass_high, own = scoped(
        "crop_grads", crop_grads, place, cotangent, (*hidden_z, hidden_core)
    )
    chip_two = (chip(2) + relayed.astype(F32)).astype(BF16)
    chip_one, chip_two, out_x, out_y, *inputs = together(chip_one, chip_two, out_x, out_y, *inputs)

    distant, nearby = over_filter(chip_two, 4, "distant"), over_filter(chip_one, 2, "nearby")
    got_x, got_y = over_dp(out_x, 1, "grad_x"), over_dp(out_y, 2, "grad_y")
    full_two = (weight_two, two_x, two_y, two_low, two_high)
    output = scoped("conv_two", conv, 1, place, (*hidden_z, hidden_core), full_two)[0]
    field_swapped = over_filter(jnp.stack(inputs), 1, "field_swap")
    distant, nearby, output, field_swapped = together(distant, nearby, output, field_swapped)

    back = chip(0) + nearby.astype(F32) + distant.astype(F32)
    sigma = jax.nn.sigmoid(pre_one)
    back_pre = (back * sigma * (1.0 + pre_one * (1.0 - sigma))).astype(BF16)
    back_all = others([back_pre] * 4, "pre")
    grad_one = scoped("grad_one_own", weight_grads, place, inputs[:1], field_swapped, back_all[:1], None, (0,))
    got_x, got_y, gate = together(got_x, got_y, back_pre)
    wide = lambda value: value.astype(F32)
    to_y = (wide(pass_low) + wide(got_x[0])).astype(BF16)
    to_x = (wide(pass_high) + wide(got_y[0])).astype(BF16)
    last_low, last_high = over_dp(to_y, 2, "grad_low"), over_dp(to_x, 1, "grad_high")
    grad_one, *back_rest = together(grad_one, *back_all[1:])
    grad_one = scoped(
        "grad_one", weight_grads, place, inputs[1:], field_swapped, back_rest, grad_one, (1, 2, 3)
    )
    half = TALL // 2
    grad_two = own + jnp.concatenate(
        [wide(got_x[1]) + wide(last_low), wide(got_y[1]) + wide(last_high)], axis=2
    )
    return (output.reshape(1, ROWS, COLS, WIDE), grad_one, grad_two)


def solution(mesh):
    n_dp, n_filter = mesh.shape["dp"], mesh.shape["filter"]

    def choose(arrays):
        fields, weights = arrays[0].shape, arrays[1].shape
        fits = (n_dp, n_filter) == (4, 8) and fields == (1, 32, 32, 128) and weights == (3, 3, 256, 128)
        return quick_body if fits else body

    placed = (
        P("dp", None, None, "filter"),
        P(None, None, "dp", "filter"),
        P(None, None, "dp", "filter"),
        P("dp", None, None, "filter"),
    )
    return jax.shard_map(
        lambda *arrays: choose(arrays)(n_dp, n_filter, *arrays),
        mesh=mesh,
        in_specs=placed,
        out_specs=(
            P("dp", None, None, "filter"),
            P(None, None, "dp", "filter"),
            P(None, None, "dp", "filter"),
        ),
        check_vma=False,
    )
```

```python
import functools

import jax
import jax.numpy as jnp
from jax import lax
from jax.experimental import pallas as pl
from jax.experimental.pallas import tpu as pltpu
from jax.sharding import PartitionSpec as P

F32, BF16 = jnp.float32, jnp.bfloat16
ANY = pl.BlockSpec(memory_space=pl.ANY)
VMEM = pl.BlockSpec(memory_space=pltpu.VMEM)
SMEM = pl.BlockSpec(memory_space=pltpu.SMEM)


def swap(values, axis, size, flip):
    return lax.ppermute(values, axis, [(i, i ^ flip) for i in range(size)])


def after(values, *earlier):
    return lax.optimization_barrier((values,) + earlier)[0]


def rank_blocks(values, axis, size, flips, dim):
    held = [(0, values)]
    for flip in flips:
        held = held + [(k ^ flip, swap(v, axis, size, flip)) for k, v in held]
    return held


def place(held, axis, dim):
    own = lax.axis_index(axis)
    width = held[0][1].shape[dim]
    shape = list(held[0][1].shape)
    shape[dim] = width * len(held)
    whole = jnp.zeros(shape, held[0][1].dtype)
    for k, piece in held:
        whole = lax.dynamic_update_slice_in_dim(whole, piece, (own ^ k) * width, dim)
    return whole


def bits(size):
    return [1 << n for n in range(size.bit_length() - 1)]


def gather_weights(weights, size):
    if size != 4:
        return place(rank_blocks(weights, "dp", size, bits(size), 2), "dp", 2)
    half = weights.shape[2] // 2
    along_x = swap(weights, "dp", size, 1)
    along_y = swap(weights, "dp", size, 2)
    far_low = swap(along_x[:, :, :half], "dp", size, 2)
    far_high = swap(along_y[:, :, half:], "dp", size, 1)
    far = jnp.concatenate([far_low, far_high], axis=2)
    return place([(0, weights), (1, along_x), (2, along_y), (3, far)], "dp", 2)


def gather_fields(values, size):
    flips = bits(size)
    held = rank_blocks(values, "filter", size, flips[:0:-1], 3)
    stacked = jnp.stack([piece for unused, piece in held])
    other = swap(stacked, "filter", size, 1)
    held = held + [(k ^ 1, other[n]) for n, (k, unused) in enumerate(held)]
    return place(held, "filter", 3)


def fold(pieces, axis, size, flip):
    keep = sorted(k for k in pieces if not k & flip)
    got = swap(jnp.stack([pieces[k | flip] for k in keep]), axis, size, flip)
    return {k: (pieces[k].astype(jnp.float32) + got[n].astype(jnp.float32)).astype(jnp.bfloat16) for n, k in enumerate(keep)}


def scatter_fields(partial, size):
    own = lax.axis_index("filter")
    width = partial.shape[3] // size
    pieces = {k: lax.dynamic_slice_in_dim(partial, (own ^ k) * width, width, 3) for k in range(size)}
    for flip in bits(size):
        pieces = fold(pieces, "filter", size, flip)
    return pieces[0].astype(jnp.float32)


def scatter_weights(partial, size):
    own = lax.axis_index("dp")
    width = partial.shape[2] // size
    pieces = {k: lax.dynamic_slice_in_dim(partial, (own ^ k) * width, width, 2) for k in range(size)}
    if size != 4:
        for flip in bits(size):
            pieces = fold(pieces, "dp", size, flip)
        return pieces[0].astype(jnp.float32)
    half = width // 2
    low = {k: v[:, :, :half] for k, v in pieces.items()}
    high = {k: v[:, :, half:] for k, v in pieces.items()}
    over_x = swap(jnp.stack([low[3], low[1]]), "dp", size, 1)
    over_y = swap(jnp.stack([high[3], high[2]]), "dp", size, 2)
    wide = lambda v: v.astype(jnp.float32)
    low_y = swap((wide(low[2]) + wide(over_x[0])).astype(jnp.bfloat16), "dp", size, 2)
    high_x = swap((wide(high[1]) + wide(over_y[0])).astype(jnp.bfloat16), "dp", size, 1)
    sum_low = wide(low[0]) + wide(over_x[1]) + wide(low_y)
    sum_high = wide(high[0]) + wide(over_y[1]) + wide(high_x)
    return jnp.concatenate([sum_low, sum_high], axis=2)


def shift_cells(values, row_step, col_step):
    size = values.shape[1]
    padded = jnp.pad(values, ((0, 0), (1, 1), (1, 1), (0, 0)))
    return padded[:, 1 + row_step : 1 + row_step + size, 1 + col_step : 1 + col_step + size, :]


def conv_taps(inputs, weights):
    products = jnp.einsum("bhwc,pqcd->bhwpqd", inputs, weights, preferred_element_type=jnp.float32)
    result = jnp.zeros(inputs.shape[:3] + (weights.shape[3],), jnp.float32)
    for row_tap in range(3):
        for col_tap in range(3):
            result = result + shift_cells(
                products[:, :, :, row_tap, col_tap, :], row_tap - 1, col_tap - 1
            )
    return result


def shifted_stack(grads):
    pieces = []
    for row_tap in range(3):
        for col_tap in range(3):
            pieces.append(shift_cells(grads, 1 - row_tap, 1 - col_tap))
    return jnp.stack(pieces, axis=3).reshape(grads.shape[:3] + (3, 3, grads.shape[3]))


def transposed(grads, weights):
    stacked = shifted_stack(grads)
    return jnp.einsum("bhwpqd,pqcd->bhwc", stacked, weights, preferred_element_type=jnp.float32)


def filter_grads(inputs, grads):
    stacked = shifted_stack(grads)
    return jnp.einsum("bhwc,bhwpqd->pqcd", inputs, stacked, preferred_element_type=jnp.float32)


def body(n_dp, n_filter, fields, weight_one, weight_two, cotangent):
    full_one = gather_weights(weight_one, n_dp)
    gathered = gather_fields(fields, n_filter)
    pre_one = conv_taps(gathered, full_one)
    hidden = jax.nn.silu(pre_one).astype(jnp.bfloat16)
    full_two = gather_weights(after(weight_two, full_one), n_dp)
    hidden_all = gather_fields(hidden, n_filter)
    partial_back = transposed(cotangent, full_two)
    output = conv_taps(hidden_all, full_two).astype(jnp.bfloat16)
    grad_two = scatter_weights(filter_grads(hidden_all, cotangent).astype(jnp.bfloat16), n_dp)
    back = scatter_fields(partial_back.astype(jnp.bfloat16), n_filter)
    sigma = jax.nn.sigmoid(pre_one)
    back_pre = (back * sigma * (1.0 + pre_one * (1.0 - sigma))).astype(jnp.bfloat16)
    grad_one = scatter_weights(filter_grads(gathered, back_pre).astype(jnp.bfloat16), n_dp)
    return (output, grad_one, grad_two)


ROWS, COLS, CELLS, WIDE, TALL, TILE = 32, 32, 1024, 128, 256, 256
TAPS = range(3)


def kernel_call(kernel, out_shape, in_specs, scratch, share, out_specs=None, aliases=None, limit=56):
    return pl.pallas_call(
        kernel,
        out_shape=out_shape,
        in_specs=in_specs,
        out_specs=out_specs or [VMEM] * len(out_shape),
        scratch_shapes=scratch,
        input_output_aliases=aliases or {},
        compiler_params=pltpu.CompilerParams(vmem_limit_bytes=limit * 2**20),
        cost_estimate=pl.CostEstimate(
            flops=int(share * 2 * 9 * CELLS * CELLS * WIDE), bytes_accessed=int(share * 2**23), transcendentals=0
        ),
    )


def bf16(*shape):
    return jax.ShapeDtypeStruct(shape, BF16)


def f32(*shape):
    return jax.ShapeDtypeStruct(shape, F32)


def column(rows):
    return lax.broadcasted_iota(jnp.int32, (rows, WIDE), 0) % COLS


def from_left(values):
    return jnp.where(column(values.shape[0]) == 0, 0.0, pltpu.roll(values, 1, 0))


def from_right(values):
    return jnp.where(column(values.shape[0]) == COLS - 1, 0.0, pltpu.roll(values, values.shape[0] - 1, 0))


def start_all(pairs, sems):
    copies = [pltpu.make_async_copy(src, dst, sems.at[n]) for n, (src, dst) in enumerate(pairs)]
    for copy in copies:
        copy.start()
    return copies


def block(index, size):
    return pl.ds(pl.multiple_of(index * size, size), size)


def weight_pairs(refs, whole, far_only=False):
    half = TALL // 2
    if far_only:
        spans = [(0, half), (half, half)]
    else:
        spans = [(0, TALL), (TALL, TALL), (2 * TALL, TALL), (3 * TALL, half), (3 * TALL + half, half)]
    return [(ref, whole.at[:, :, pl.ds(*span), :]) for ref, span in zip(refs, spans)]


def field_pairs(place, refs, whole):
    pieces = [*refs[:4], *([refs[4].at[n] for n in range(4)] if len(refs) == 5 else refs[4:])]
    pairs = []
    for flip, ref in zip((0, 2, 4, 6, 1, 3, 5, 7), pieces):
        channels = place[0] ^ flip
        spot = (((channels >> 1) ^ place[1]) << 1) + (channels & 1)
        pairs.append((ref, whole.at[pl.ds(COLS, CELLS), block(spot, WIDE)]))
    return pairs


def clear_edges(held):
    edge = jnp.zeros((COLS, held.shape[1]), BF16)
    held[:COLS, :] = edge
    held[COLS + CELLS :, :] = edge


def taps_sum(held, taps, depth, start):
    sums = None
    for p in TAPS:
        across = jnp.concatenate([taps[p, q, :depth] for q in TAPS], axis=1)
        begin = start + p * COLS
        part = jnp.dot(held[begin : begin + TILE, :depth], across, preferred_element_type=F32)
        sums = part if sums is None else sums + part
    return sums[:, WIDE : 2 * WIDE] + from_left(sums[:, :WIDE]) + from_right(sums[:, 2 * WIDE :])


def conv_kernel(layer, count, place, *refs):
    outs = refs[-5:-3] if layer == 0 else refs[-4:-3]
    fields, weights, (held, taps, sems) = refs[:count], refs[count : -3 - len(outs)], refs[-3:]
    copies = start_all(field_pairs(place, fields, held) + weight_pairs(weights, taps), sems)
    clear_edges(held)
    for copy in copies:
        copy.wait()
    for start in range(0, CELLS, TILE):
        rows = slice(start, start + TILE)
        total = taps_sum(held, taps, 4 * TALL, start)
        if layer == 0:
            outs[0][rows, :] = total
            outs[1][rows, :] = (total / (1.0 + jnp.exp(-total))).astype(BF16)
        else:
            outs[0][rows, :] = total.astype(BF16)


def conv(layer, place, fields, weights):
    return kernel_call(
        functools.partial(conv_kernel, layer, len(fields)),
        ([f32(CELLS, WIDE)] if layer == 0 else []) + [bf16(CELLS, WIDE)],
        [SMEM] + [ANY] * (len(fields) + 5),
        [
            pltpu.VMEM((CELLS + 2 * COLS, 4 * TALL), BF16),
            pltpu.VMEM((3, 3, 4 * TALL, WIDE), BF16),
            pltpu.SemaphoreType.DMA((13,)),
        ],
        1,
    )(place, *fields, *weights)


def spread(values, shifted):
    clear_edges(shifted)
    wide = values.astype(F32)
    inside = slice(COLS, COLS + CELLS)
    shifted[inside, :WIDE] = from_right(wide).astype(BF16)
    shifted[inside, WIDE : 2 * WIDE] = values
    shifted[inside, 2 * WIDE :] = from_left(wide).astype(BF16)


def back_tile(shifted, taps, first, start, odd):
    across = jnp.concatenate([taps[p, q, first : first + TALL, :] for p in TAPS for q in TAPS], axis=1)
    begins = [start + (2 - p) * COLS for p in TAPS]
    stacked = jnp.concatenate([shifted[begin : begin + TILE, :] for begin in begins], axis=1)
    sums = lax.dot_general(stacked, across, (((1,), (1,)), ((), ())), preferred_element_type=F32)
    even_part, odd_part = sums[:, :WIDE], sums[:, WIDE:]
    return jnp.where(odd, odd_part, even_part).astype(BF16), jnp.where(odd, even_part, odd_part).astype(BF16)


def back_near_kernel(place, grads, own, along_x, along_y, keep, send, shifted, taps, sems):
    copies = start_all(weight_pairs((own, along_x, along_y), taps), sems)
    spread(grads[...], shifted)
    for copy in copies:
        copy.wait()
    odd = (place[0] & 1) == 1
    for k in range(3):
        slot = (place[0] >> 1) ^ place[1] ^ k
        for start in range(0, CELLS, TILE):
            rows = slice(start, start + TILE)
            keep[slot, rows, :], send[slot, rows, :] = back_tile(shifted, taps, k * TALL, start, odd)


def back_near(place, grads, weights):
    return kernel_call(
        back_near_kernel,
        [bf16(4, CELLS, WIDE)] * 2,
        [SMEM, VMEM] + [ANY] * 3,
        [
            pltpu.VMEM((CELLS + 2 * COLS, 3 * WIDE), BF16),
            pltpu.VMEM((3, 3, 3 * TALL, WIDE), BF16),
            pltpu.SemaphoreType.DMA((3,)),
        ],
        0.75,
    )(place, grads, *weights)


def back_far_kernel(place, grads, low, high, keep_in, send_in, keep, send, parts, shifted, taps, sems):
    copies = start_all(weight_pairs((low, high), taps, True), sems)
    spread(grads[...], shifted)
    for copy in copies:
        copy.wait()
    odd = (place[0] & 1) == 1
    slot = (place[0] >> 1) ^ place[1] ^ 3
    for start in range(0, CELLS, TILE):
        rows = slice(start, start + TILE)
        parts[0, rows, :], parts[1, rows, :] = back_tile(shifted, taps, 0, start, odd)
    outward = [pltpu.make_async_copy(parts.at[n], ref.at[slot], sems.at[2 + n]) for n, ref in enumerate((keep, send))]
    for copy in outward:
        copy.start()
    for copy in outward:
        copy.wait()


def back_far(place, grads, weights, keep, send):
    return kernel_call(
        back_far_kernel,
        [bf16(4, CELLS, WIDE)] * 2,
        [SMEM, VMEM] + [ANY] * 4,
        [
            pltpu.VMEM((2, CELLS, WIDE), BF16),
            pltpu.VMEM((CELLS + 2 * COLS, 3 * WIDE), BF16),
            pltpu.VMEM((3, 3, TALL, WIDE), BF16),
            pltpu.SemaphoreType.DMA((4,)),
        ],
        0.25,
        [ANY, ANY],
        {4: 0, 5: 1},
    )(place, grads, *weights, keep, send)


def tap_grads(fields, shifted):
    stacked = jnp.concatenate([shifted[(2 - p) * COLS : (2 - p) * COLS + CELLS, :] for p in TAPS], axis=1)
    sums = lax.dot_general(fields, stacked, (((0,), (0,)), ((), ())), preferred_element_type=F32)
    return lambda p, q: sums[:, (3 * p + q) * WIDE : (3 * p + q + 1) * WIDE]


def crop_grad_kernel(count, place, grads, *refs):
    fields, (out_x, out_y, pass_low, pass_high, own, held, shifted, sems) = refs[:count], refs[count:]
    copies = start_all(field_pairs(place, fields, held), sems)
    spread(grads[...], shifted)
    for copy in copies:
        copy.wait()
    half = TALL // 2
    targets = {3: (out_x.at[0], out_y.at[0]), 1: (out_x.at[1], pass_high), 2: (pass_low, out_y.at[1])}
    for k in (3, 1, 2, 0):
        sums = tap_grads(held[COLS : COLS + CELLS, k * TALL : (k + 1) * TALL], shifted)
        for p in TAPS:
            for q in TAPS:
                part = sums(p, q)
                if k == 0:
                    own[p, q] = part
                else:
                    low, high = targets[k]
                    low[p, q] = part[:half].astype(BF16)
                    high[p, q] = part[half:].astype(BF16)


def crop_grads(place, grads, fields):
    half = TALL // 2
    return kernel_call(
        functools.partial(crop_grad_kernel, len(fields)),
        [bf16(2, 3, 3, half, WIDE)] * 2 + [bf16(3, 3, half, WIDE)] * 2 + [f32(3, 3, TALL, WIDE)],
        [SMEM, VMEM] + [ANY] * len(fields),
        [
            pltpu.VMEM((CELLS + 2 * COLS, 4 * TALL), BF16),
            pltpu.VMEM((CELLS + 2 * COLS, 3 * WIDE), BF16),
            pltpu.SemaphoreType.DMA((8,)),
        ],
        1,
    )(place, grads, *fields)


def grad_kernel(slots, adds, place, *refs):
    count = len(slots)
    mine, other, grads = refs[:count], refs[count], refs[count + 1 : 2 * count + 1]
    before = refs[2 * count + 1] if adds else None
    out, held, cots, shifted, sems = refs[2 * count + 1 + adds :]
    core = place[0] & 1
    pairs = []
    for n, slot in enumerate(slots):
        pairs.append((mine[n], held.at[n, :, block(core, WIDE)]))
        pairs.append((other.at[slot], held.at[n, :, block(1 - core, WIDE)]))
        pairs.append((grads[n], cots.at[n]))
    copies = start_all(pairs, sems)
    for n in range(count):
        for copy in copies[3 * n : 3 * n + 3]:
            copy.wait()
        spread(cots[n], shifted)
        sums = tap_grads(held[n], shifted)
        for p in TAPS:
            for q in TAPS:
                earlier = before if n == 0 else out
                out[p, q] = sums(p, q) if earlier is None else earlier[p, q] + sums(p, q)


def weight_grads(place, mine, other, grads, before, slots):
    count = len(slots)
    adds = 0 if before is None else 1
    return kernel_call(
        functools.partial(grad_kernel, slots, adds),
        [f32(3, 3, TALL, WIDE)],
        [SMEM] + [ANY] * (2 * count + 1) + [VMEM] * adds,
        [
            pltpu.VMEM((count, CELLS, TALL), BF16),
            pltpu.VMEM((count, CELLS, WIDE), BF16),
            pltpu.VMEM((CELLS + 2 * COLS, 3 * WIDE), BF16),
            pltpu.SemaphoreType.DMA((3 * count,)),
        ],
        count / 4,
        limit=20,
    )(place, *mine, other, *grads, *([] if before is None else [before]))[0]


def over_dp(values, flip, name):
    with jax.named_scope(name):
        return swap(values, "dp", 4, flip)


def over_filter(values, flip, name):
    with jax.named_scope(name):
        return swap(values, "filter", 8, flip)


def together(*values):
    return lax.optimization_barrier(values)


def others(pieces, name):
    return [pieces[0]] + [over_dp(pieces[k], k, name + str(k)) for k in (1, 2, 3)]


def pick(pieces, index):
    chosen = pieces[0]
    for n in (1, 2, 3):
        chosen = jnp.where(index == n, pieces[n], chosen)
    return chosen


def scoped(name, function, *arguments):
    with jax.named_scope(name):
        return function(*arguments)


def quick_body(n_dp, n_filter, fields, weight_one, weight_two, cotangent):
    own_filter, own_dp = lax.axis_index("filter"), lax.axis_index("dp")
    place = jnp.stack([own_filter, own_dp]).astype(jnp.int32)
    owner = own_dp ^ (own_filter >> 1)
    fields, cotangent = fields.reshape(CELLS, WIDE), cotangent.reshape(CELLS, WIDE)

    half = TALL // 2

    def far_weights(along_x, along_y, name):
        return over_dp(along_x[:, :, :half], 2, name + "_low"), over_dp(along_y[:, :, half:], 1, name + "_high")

    one_x, one_y = over_dp(weight_one, 1, "one_x"), over_dp(weight_one, 2, "one_y")
    field_near, field_far = over_filter(fields, 2, "field_near"), over_filter(fields, 4, "field_far")
    field_core0 = over_filter(fields, 1, "field_core0")
    field_near, field_far, one_x, one_y, field_core0, place = together(
        field_near, field_far, one_x, one_y, field_core0, place)
    one_low, one_high = far_weights(one_x, one_y, "one")
    field_last = over_filter(field_far, 2, "field_last")
    field_core1, field_core2 = over_filter(field_near, 1, "field_core1"), over_filter(field_far, 1, "field_core2")
    field_last, field_core1, field_core2, one_low, one_high, weight_gated = together(
        field_last, field_core1, field_core2, one_low, one_high, weight_two)
    field_core3 = over_filter(field_last, 1, "field_core3")
    field_z = (fields, field_near, field_far, field_last)
    two_x, two_y = over_dp(weight_gated, 1, "two_x"), over_dp(weight_gated, 2, "two_y")
    pre_one, hidden = scoped(
        "conv_one", conv, 0, place, (*field_z, field_core0, field_core1, field_core2, field_core3),
        (weight_one, one_x, one_y, one_low, one_high)
    )
    hidden_far, hidden_near = over_filter(hidden, 4, "hidden_far"), over_filter(hidden, 2, "hidden_near")
    two_x, two_y, gate, *field_z = together(two_x, two_y, hidden, *field_z)

    two_low, two_high = far_weights(two_x, two_y, "two")
    keep, send = scoped("back_near", back_near, place, cotangent, (weight_two, two_x, two_y))
    inputs = [pick(field_z, owner ^ k) for k in range(4)]
    two_low, two_high, keep, send, hidden_far, hidden_near, *inputs = together(
        two_low, two_high, keep, send, hidden_far, hidden_near, *inputs
    )

    inputs = others(inputs, "input")
    hidden_last = over_filter(hidden_far, 2, "hidden_last")
    keep, send = scoped("back_far", back_far, place, cotangent, (two_low, two_high), keep, send)
    keep, send, hidden_last = together(keep, send, hidden_last)
    got = over_filter(send, 1, "back_core")
    chip = lambda n: keep[n].astype(F32) + got[n].astype(F32)
    chip_one, chip_three = chip(1).astype(BF16), chip(3).astype(BF16)
    relayed = over_filter(chip_three, 2, "relayed")
    hidden_z = (hidden, hidden_near, hidden_far, hidden_last)
    hidden_core = over_filter(jnp.stack(hidden_z), 1, "hidden_core")
    out_x, out_y, pass_low, pass_high, own = scoped(
        "crop_grads", crop_grads, place, cotangent, (*hidden_z, hidden_core)
    )
    chip_two = (chip(2) + relayed.astype(F32)).astype(BF16)
    chip_one, chip_two, out_x, out_y, *inputs = together(chip_one, chip_two, out_x, out_y, *inputs)

    distant, nearby = over_filter(chip_two, 4, "distant"), over_filter(chip_one, 2, "nearby")
    got_x, got_y = over_dp(out_x, 1, "grad_x"), over_dp(out_y, 2, "grad_y")
    full_two = (weight_two, two_x, two_y, two_low, two_high)
    output = scoped("conv_two", conv, 1, place, (*hidden_z, hidden_core), full_two)[0]
    field_swapped = over_filter(jnp.stack(inputs), 1, "field_swap")
    distant, nearby, output, field_swapped = together(distant, nearby, output, field_swapped)

    back = chip(0) + nearby.astype(F32) + distant.astype(F32)
    sigma = jax.nn.sigmoid(pre_one)
    back_pre = (back * sigma * (1.0 + pre_one * (1.0 - sigma))).astype(BF16)
    back_all = others([back_pre] * 4, "pre")
    grad_one = scoped("grad_one_own", weight_grads, place, inputs[:1], field_swapped, back_all[:1], None, (0,))
    got_x, got_y, gate = together(got_x, got_y, back_pre)
    wide = lambda value: value.astype(F32)
    to_y = (wide(pass_low) + wide(got_x[0])).astype(BF16)
    to_x = (wide(pass_high) + wide(got_y[0])).astype(BF16)
    last_low, last_high = over_dp(to_y, 2, "grad_low"), over_dp(to_x, 1, "grad_high")
    grad_one, *back_rest = together(grad_one, *back_all[1:])
    grad_one = scoped(
        "grad_one", weight_grads, place, inputs[1:], field_swapped, back_rest, grad_one, (1, 2, 3)
    )
    half = TALL // 2
    grad_two = own + jnp.concatenate(
        [wide(got_x[1]) + wide(last_low), wide(got_y[1]) + wide(last_high)], axis=2
    )
    return (output.reshape(1, ROWS, COLS, WIDE), grad_one, grad_two)


def solution(mesh):
    n_dp, n_filter = mesh.shape["dp"], mesh.shape["filter"]

    def choose(arrays):
        fields, weights = arrays[0].shape, arrays[1].shape
        fits = (n_dp, n_filter) == (4, 8) and fields == (1, 32, 32, 128) and weights == (3, 3, 256, 128)
        return quick_body if fits else body

    placed = (
        P("dp", None, None, "filter"),
        P(None, None, "dp", "filter"),
        P(None, None, "dp", "filter"),
        P("dp", None, None, "filter"),
    )
    return jax.shard_map(
        lambda *arrays: choose(arrays)(n_dp, n_filter, *arrays),
        mesh=mesh,
        in_specs=placed,
        out_specs=(
            P("dp", None, None, "filter"),
            P(None, None, "dp", "filter"),
            P(None, None, "dp", "filter"),
        ),
        check_vma=False,
    )
```
